128 devices in a mesh: sub: 8 (over z, core), leaf: 16 (over y, x).
Axes of the slice: x: 4, y: 4, z: 4, core: 2. Of those that a mesh axis runs over, the one named last changes fastest.
Arguments:
- tiles: bfloat16 [512, 128, 128], replicated, may hold values from -0.5 to 0.5
- tile_rows: int32 [512], replicated, may hold values from 0 to 511, as said below
- tile_cols: int32 [512], replicated, may hold values from 0 to 1023
- cost: bfloat16 [512, 131072], P(('sub', 'leaf')), may hold values from -6 to 6
- demand: bfloat16 [512, 65536], P(('sub', 'leaf')), may hold values from -6 to 6
- upper: float32 [131072], replicated, may hold values from 0.5 to 4
- prob: float32 [512], P(('sub', 'leaf')), may hold values from 0.01 to 1
- node_of_scen: int32 [512], P(('sub', 'leaf')), may hold values from 0 to 127, as said below
- root_blocks: int32 [512], replicated, may hold values from 0 to 1023, as said below
- node_blocks: int32 [128, 128], replicated, may hold values from 0 to 1023, as said below
Outputs:
- primal: float32 [512, 131072], P(('sub', 'leaf'))
- dual: float32 [512, 65536], P(('sub', 'leaf'))
- multiplier: float32 [512, 131072], P(('sub', 'leaf'))
The draws below stay inside these ranges and needn't reach their ends.
Inputs may be any that keep to these rules, and one draw needn't show every extreme that they name: `tile_rows`: each of the 512 row blocks is named by exactly 1 tiles. `node_of_scen`: scenario s belongs to a node of group g = (s // 4) % 16, numbered g * 8 to g * 8 + 7; every node has at least one scenario; node sizes are uneven. `root_blocks`: distinct block indices. `node_blocks`: each row holds 128 distinct block indices, none of them in root_blocks.
All inputs are finite; a program needn't handle non-finite values.
Results may differ from the reference program's by a relative error of at most 0.00088.
Values sent between devices are 32-bit elements; how exact they have to be, the bound alone decides.
A program may use at most 128 MiB of HBM per device.

```python
import math
import jax
import jax.numpy as jnp

TILE = 128
NVAR = 131072
NCON = 65536
NT = 512
NB_ROOT = 512
NB = 128
NPG = 8
S_DEV = 4
PH_ITERS = 2
PD_STEPS = 2
NVT = 1024
NCT = 512
SCEN = 512
NODES = 128


def block_order(key):
    return jax.random.permutation(jax.random.fold_in(key, 11), NVT)


def draw_root_blocks(key, part):
    return block_order(key)[:NB_ROOT].astype(jnp.int32)


def draw_node_blocks(key, part):
    pool = block_order(key)[NB_ROOT:]
    node_keys = jax.random.split(jax.random.fold_in(key, 13), NODES)
    picks = jax.vmap(lambda one_key: jax.random.permutation(one_key, NVT - NB_ROOT)[:NB])(node_keys)
    return pool[picks].astype(jnp.int32)


def draw_tile_rows(key, part):
    order = jax.random.permutation(jax.random.fold_in(key, 17), NT)
    return (order % NCT).astype(jnp.int32)


def draw_node_of_scen(key, part):
    groups = NODES // NPG
    per_group = SCEN // groups
    scen_index = jnp.arange(SCEN)
    device_block = scen_index // S_DEV
    group = device_block % groups
    position = device_block // groups * S_DEV + scen_index % S_DEV
    group_keys = jax.random.split(jax.random.fold_in(key, 19), groups)
    ranks = jax.vmap(lambda one_key: jax.random.permutation(one_key, per_group))(group_keys)
    rank = ranks[group, position]
    first_pick = jax.random.randint(jax.random.fold_in(key, 23), (SCEN,), 0, NPG)
    second_pick = jax.random.randint(jax.random.fold_in(key, 29), (SCEN,), 0, NPG)
    skewed = jnp.minimum(first_pick, second_pick)
    local_node = jnp.where(rank < NPG, rank, skewed)
    return (group * NPG + local_node).astype(jnp.int32)


def plant(entries, stream_key, low, high):
    index_at = [jax.random.randint(jax.random.fold_in(stream_key, axis), (), 0, length) for axis, length in enumerate(entries.shape)]
    longest = entries.shape.index(max(entries.shape))
    neighbour = index_at[:longest] + [(index_at[longest] + 1) % entries.shape[longest]] + index_at[longest + 1:]
    return entries.at[tuple(index_at)].set(low).at[tuple(neighbour)].set(high)


def block_scale(key, dims, pieces, smallest, top_value):
    def one(dim, parts):
        steps = jax.random.uniform(jax.random.fold_in(jax.random.fold_in(key, 6), dim), (parts,), jnp.float32, smallest / len(pieces), top_value / len(pieces))
        return jnp.repeat(jnp.exp(steps), dims[dim] // parts).reshape((-1,) + (1,) * (len(dims) - dim - 1))

    factor_of = one(*pieces[0])
    for cut in pieces[1:]:
        factor_of = factor_of * one(*cut)
    return factor_of


def gaussian(stream_key, extent, deviation, reach, cuts=(), dtype=jnp.bfloat16):
    drawn = jax.random.normal(stream_key, extent, jnp.float32) * deviation
    if len(cuts) > 0:
        drawn = block_scale(stream_key, extent, cuts, -0.22, 0.18) * drawn
    return jnp.clip(drawn, min=-reach, max=reach).astype(dtype)


def setup_inputs(seed: int = 0) -> dict:
    seeds = jax.random.split(jax.random.key(seed), 11)
    tiles = gaussian(seeds[0], (NT, TILE, TILE), TILE ** -0.5, 0.5)
    tile_rows = draw_tile_rows(jax.random.fold_in(seeds[10], 71), 0)
    tile_cols = plant(jax.random.randint(seeds[2], (NT,), 0, NVT), jax.random.fold_in(seeds[2], 1), 0, NVT - 1).astype(jnp.int32)
    cost = gaussian(seeds[3], (SCEN, NVAR), 1.0, 6.0, ((0, 128),))
    demand = gaussian(seeds[4], (SCEN, NCON), 1.0, 6.0, ((0, 128),))
    upper = jnp.clip(jnp.exp(jax.random.uniform(seeds[5], (NVAR,), jnp.float32, math.log(0.5), math.log(4.0))), 0.5, 4.0)
    prob = jnp.clip(jnp.exp(math.log(1.0) - 4.6051702 * jax.random.uniform(seeds[6], (SCEN,), jnp.float32) ** block_scale(seeds[6], (SCEN,), ((0, 128),), -0.2, 0.2)), 0.01, 1.0)
    node_of_scen = draw_node_of_scen(jax.random.fold_in(seeds[10], 71), 0)
    root_blocks = draw_root_blocks(jax.random.fold_in(seeds[10], 71), 0)
    node_blocks = draw_node_blocks(jax.random.fold_in(seeds[10], 71), 0)
    return {"tiles": tiles, "tile_rows": tile_rows, "tile_cols": tile_cols, "cost": cost, "demand": demand, "upper": upper, "prob": prob, "node_of_scen": node_of_scen, "root_blocks": root_blocks, "node_blocks": node_blocks}


primal_step = 1.0
dual_step = 0.25
penalty = 1.0


def apply_matrix(tiles, tile_rows, tile_cols, field16):
    count = field16.shape[0]
    blocks = field16.reshape(count, NVT, TILE)[:, tile_cols, :]
    terms = jnp.einsum("snk,nrk->nsr", blocks.astype(jnp.float32), tiles.astype(jnp.float32))
    summed = jax.ops.segment_sum(terms, tile_rows, num_segments=NCT)
    return jnp.transpose(summed, (1, 0, 2)).reshape(count, NCON)


def apply_transpose(tiles, tile_rows, tile_cols, field16):
    count = field16.shape[0]
    blocks = field16.reshape(count, NCT, TILE)[:, tile_rows, :]
    terms = jnp.einsum("snr,nrk->nsk", blocks.astype(jnp.float32), tiles.astype(jnp.float32))
    summed = jax.ops.segment_sum(terms, tile_cols, num_segments=NVT)
    return jnp.transpose(summed, (1, 0, 2)).reshape(count, NVAR)


def reference(tiles, tile_rows, tile_cols, cost, demand, upper, prob, node_of_scen, root_blocks, node_blocks):
    cost_f = cost.astype(jnp.float32)
    demand_f = demand.astype(jnp.float32)
    primal = jnp.zeros((SCEN, NVAR), jnp.float32)
    dual = jnp.zeros((SCEN, NCON), jnp.float32)
    multiplier = jnp.zeros((SCEN, NVAR), jnp.float32)
    consensus = jnp.zeros((SCEN, NVAR), jnp.float32)
    scen_index = jnp.arange(SCEN)[:, None]
    own_blocks = node_blocks[node_of_scen]
    for outer in range(PH_ITERS):
        for inner in range(PD_STEPS):
            gradient = apply_transpose(tiles, tile_rows, tile_cols, dual.astype(jnp.bfloat16))
            moved = primal - primal_step * (cost_f + multiplier - gradient) + primal_step * penalty * consensus
            nextval = jnp.clip(moved / (1.0 + primal_step * penalty), 0.0, upper[None, :])
            extrap = (2.0 * nextval - primal).astype(jnp.bfloat16)
            dual = jnp.maximum(dual + dual_step * (demand_f - apply_matrix(tiles, tile_rows, tile_cols, extrap)), 0.0)
            primal = nextval
        shaped = primal.reshape(SCEN, NVT, TILE)
        root_vals = shaped[:, root_blocks, :]
        root_mean = jnp.sum(prob[:, None, None] * root_vals, axis=0) / jnp.sum(prob)
        node_vals = shaped[scen_index, own_blocks]
        node_sum = jax.ops.segment_sum(prob[:, None, None] * node_vals, node_of_scen, num_segments=NODES)
        node_weight = jax.ops.segment_sum(prob, node_of_scen, num_segments=NODES)
        node_mean = node_sum / node_weight[:, None, None]
        merged = shaped.at[:, root_blocks, :].set(jnp.broadcast_to(root_mean, (SCEN, NB_ROOT, TILE)))
        merged = merged.at[scen_index, own_blocks].set(node_mean[node_of_scen])
        consensus = merged.reshape(SCEN, NVAR)
        multiplier = multiplier + penalty * (primal - consensus)
    return primal, dual, multiplier
```

```python
import functools

import jax
import jax.numpy as jnp
from jax import lax
from jax.experimental import pallas as pl
from jax.experimental.pallas import tpu as pltpu
from jax.sharding import PartitionSpec as P

F32 = jnp.float32
BF16 = jnp.bfloat16
MESH = pl.DeviceIdType.MESH
LANES = 128
PAD = 8


def aligned(value, step=8):
    return pl.multiple_of(value, step)


def top_rows():
    return lax.broadcasted_iota(jnp.int32, (8, LANES), 0) < 4


def unroll_of(count, most):
    step = min(count, most)
    while count % step:
        step -= 1
    return step


def loop(count, most, body, carry=0):
    step = unroll_of(count, most)

    def outer(i, state):
        for u in range(step):
            state = body(i * step + u, state)
        return state

    return lax.fori_loop(0, count // step, outer, carry)


def start_tiles(tiles_hbm, tiles, sems, chunks):
    size = tiles.shape[0] // chunks
    for c in range(chunks):
        part = pl.ds(c * size, size)
        pltpu.make_async_copy(tiles_hbm.at[part], tiles.at[part], sems.at[c]).start()


def wait_tiles(tiles_hbm, tiles, sems, chunks, c):
    size = tiles.shape[0] // chunks
    part = pl.ds(c * size, size)
    pltpu.make_async_copy(tiles_hbm.at[part], tiles.at[part], sems.at[c]).wait()


def pick_pair(ref, first4, second4):
    low = ref[pl.ds(first4 + PAD, 8), :]
    high = ref[pl.ds(second4 + (PAD - 4), 8), :]
    return jnp.where(top_rows(), low, high)


def spread_upper(upper, wide):
    blocks = upper.shape[0]
    for s in range(4):
        wide[pl.ds(s, blocks, stride=4), :] = upper[...]


def pairs_a(tiles, cols4, field, pairs, emit, most):
    def body(p, state):
        lhs = pick_pair(field, cols4[2 * p], cols4[2 * p + 1]).astype(BF16)
        rhs = tiles[pl.ds(2 * p, 2)].reshape(2 * LANES, LANES)
        both = lax.dot_general(lhs, rhs, (((1,), (1,)), ((), ())), preferred_element_type=F32)
        emit(p, jnp.where(top_rows(), both[:, :LANES], both[:, LANES:]))
        return state

    first, count = pairs
    step = unroll_of(count, most)

    def outer(i, state):
        for u in range(step):
            body(first + i * step + u, state)
        return state

    lax.fori_loop(0, count // step, outer, 0)


def transpose_pass(tiles, order, order4, follows, dual, sums, most):
    pairs = tiles.shape[0] // 2
    zero = jnp.zeros((8, LANES), F32)
    sums[pl.ds(PAD + 8 * pairs, 8), :] = zero

    def body(p, carry):
        a, b = 2 * p, 2 * p + 1
        top = top_rows()
        low = dual[pl.ds(order4[a] + PAD, 8), :]
        high = dual[pl.ds(order4[b] + (PAD - 4), 8), :]
        lhs = jnp.concatenate([jnp.where(top, low, 0.0), jnp.where(top, 0.0, high)], axis=1)
        rhs = jnp.concatenate([tiles[order[a]], tiles[order[b]]], axis=0)
        own = lax.dot_general(
            lhs.astype(BF16), rhs, (((1,), (0,)), ((), ())), preferred_element_type=F32
        )
        fa, fb = follows[a], follows[b]
        other = pltpu.roll(own, 4, 0)
        within = own + jnp.where(top, 0.0, fb) * other
        full = jnp.where(top, fb * own + other, within)
        both = fa * fb
        sums[pl.ds(aligned(PAD + 8 * p), 8), :] = within + jnp.where(top, fa, both) * carry
        return both * carry + full

    loop(pairs, most, body, zero)


def first_step(cost, wide, field):
    rows = cost.shape[0]

    def body(i, state):
        at = aligned(16 * i, 16)
        moved = -cost[pl.ds(at, 16), :].astype(F32) * 0.5
        field[pl.ds(at + PAD, 16), :] = 2.0 * jnp.clip(moved, 0.0, wide[pl.ds(at, 16), :])
        return state

    loop(rows // 16, 8, body)


def later_step(cost, wide, sums, last4, base, primal_out, field, old):
    rows = cost.shape[0]

    def body(i, state):
        at = aligned(16 * i, 16)
        gradient = jnp.concatenate(
            [
                pick_pair(sums, last4[4 * i], last4[4 * i + 1]),
                pick_pair(sums, last4[4 * i + 2], last4[4 * i + 3]),
            ],
            axis=0,
        )
        before = old(at)
        moved = base(at, before) - cost[pl.ds(at, 16), :].astype(F32) + gradient
        after = jnp.clip(moved * 0.5, 0.0, wide[pl.ds(at, 16), :])
        primal_out[pl.ds(at, 16), :] = after
        field[pl.ds(at + PAD, 16), :] = 2.0 * after - before
        return state

    loop(rows // 16, 8, body)


def weigh(primal, prob, node_of, root_blocks, node_blocks, group, total, vals, root_part, node_part):
    blocks = total.shape[0]
    acc = prob[0] * primal[pl.ds(0, blocks, stride=4), :]
    for s in range(1, 4):
        acc = acc + prob[s] * primal[pl.ds(s, blocks, stride=4), :]
    total[...] = acc

    root_count = root_blocks.shape[0]
    pieces = (root_part.shape[0] - root_count) // 8
    each = root_count // pieces
    split = each + 8

    def root_body(i, state):
        for u in range(each):
            row = total[pl.ds(root_blocks[i * each + u], 1), :]
            root_part[pl.ds(i * split + u, 1), :] = row
        weight = prob[0] + prob[1] + prob[2] + prob[3]
        root_part[pl.ds(i * split + each, 8), :] = jnp.full((8, LANES), weight, F32)
        return state

    lax.fori_loop(0, pieces, root_body, 0)

    width = node_blocks.shape[1]
    for s in range(4):

        def node_body(b, state):
            row = primal[pl.ds(4 * node_blocks[node_of[s], b] + s, 1), :]
            vals[pl.ds(s * width + b, 1), :] = row
            return state

        loop(width, 16, node_body)

    nodes = node_part.shape[0] // (width + 8)
    for m in range(nodes):
        slot = (m % 2) * (nodes // 2) + m // 2
        share = [
            jnp.where(node_of[s] == group * nodes + m, prob[s], 0.0) for s in range(4)
        ]
        part = share[0] * vals[pl.ds(0, width), :]
        for s in range(1, 4):
            part = part + share[s] * vals[pl.ds(s * width, width), :]
        node_part[pl.ds(slot * (width + 8), width), :] = part
        node_part[pl.ds(slot * (width + 8) + width, 8), :] = jnp.full(
            (8, LANES), share[0] + share[1] + share[2] + share[3], F32
        )


def split_two(value):
    high = value.astype(BF16)
    low = (value - high.astype(F32)).astype(BF16)
    return jnp.concatenate([high, low], axis=1)


def fill_means(root_mean, node_mean, root_row, node_row, node_of, group, filled, mask):
    blocks = filled.shape[0] // 4
    chunk = min(blocks, 256)
    width = node_mean.shape[0] // 8
    ones_root = jnp.ones((root_mean.shape[0], LANES), BF16)
    ones_node = jnp.ones((width, LANES), BF16)
    root_rhs = split_two(root_mean[...])
    node_rhs = []
    for s in range(4):
        m = node_of[s] - group * 8
        slot = (m % 2) * 4 + m // 2
        node_rhs.append(split_two(node_mean[pl.ds(aligned(slot * width), width), :]))
    for i in range(blocks // chunk):
        here = lax.broadcasted_iota(jnp.int32, (chunk, root_row.shape[1]), 0) + i * chunk
        hot = (here == root_row[...]).astype(F32).astype(BF16)
        got = jnp.dot(hot, root_rhs, preferred_element_type=F32)
        root_fill = got[:, :LANES] + got[:, LANES:]
        root_mask = jnp.dot(hot, ones_root, preferred_element_type=F32)
        here = lax.broadcasted_iota(jnp.int32, (chunk, width), 0) + i * chunk
        for s in range(4):
            hot = (here == node_row[pl.ds(node_of[s], 1), :]).astype(F32).astype(BF16)
            got = jnp.dot(hot, node_rhs[s], preferred_element_type=F32)
            rows = pl.ds(4 * i * chunk + s, chunk, stride=4)
            filled[rows, :] = root_fill + got[:, :LANES] + got[:, LANES:]
            mask[rows, :] = root_mask + jnp.dot(hot, ones_node, preferred_element_type=F32)


def first_kernel(
    chunks, most,
    cols4, rows4, order, order4, follows, last4, prob, node_of, root_blocks, node_blocks,
    tiles_hbm, cost, demand, upper,
    primal_out, dual_out, sums_out, demand_out, wide_out, root_part, node_part,
    tiles, field, total, vals, demand_f, sems,
):
    group = lax.axis_index("leaf")
    start_tiles(tiles_hbm, tiles, sems, chunks)
    spread_upper(upper, wide_out)
    demand_f[pl.ds(PAD, demand.shape[0]), :] = demand[...].astype(F32)
    first_step(cost, wide_out, field)
    pairs = tiles.shape[0] // 2
    per_chunk = pairs // chunks

    def emit_first(p, image):
        want = pick_pair(demand_f, rows4[2 * p], rows4[2 * p + 1])
        demand_out[pl.ds(aligned(8 * p), 8), :] = want
        dual_out[pl.ds(aligned(PAD + 8 * p), 8), :] = jnp.maximum(0.25 * (want - image), 0.0)

    def chunk_body(c, state):
        wait_tiles(tiles_hbm, tiles, sems, chunks, c)
        pairs_a(tiles, cols4, field, (c * per_chunk, per_chunk), emit_first, most)
        return state

    lax.fori_loop(0, chunks, chunk_body, 0)
    transpose_pass(tiles, order, order4, follows, dual_out, sums_out, most)
    later_step(
        cost, wide_out, sums_out, last4,
        lambda at, before: before, primal_out, field,
        lambda at: 0.5 * field[pl.ds(at + PAD, 16), :],
    )
    weigh(primal_out, prob, node_of, root_blocks, node_blocks, group, total, vals, root_part, node_part)

    def emit_next(p, image):
        at = aligned(8 * p)
        old = dual_out[pl.ds(at + PAD, 8), :]
        dual_out[pl.ds(at + PAD, 8), :] = jnp.maximum(
            old + 0.25 * (demand_out[pl.ds(at, 8), :] - image), 0.0
        )

    pairs_a(tiles, cols4, field, (0, pairs), emit_next, most)
    transpose_pass(tiles, order, order4, follows, dual_out, sums_out, most)


def second_kernel(
    chunks, most,
    cols4, order, order4, follows, last4, inverse4, prob, node_of, root_blocks, node_blocks,
    tiles_hbm, cost, wide, demand_n, primal_in, dual_in, sums, root_mean, node_mean, root_row, node_row,
    primal_out, dual_final, rest_out, root_part, node_part,
    tiles, field, total, vals, dual, sums_next, filled, mask, third, sems,
):
    group = lax.axis_index("leaf")
    start_tiles(tiles_hbm, tiles, sems, chunks)
    fill_means(root_mean, node_mean, root_row, node_row, node_of, group, filled, mask)
    rows = primal_in.shape[0]
    pairs = tiles.shape[0] // 2
    per_chunk = pairs // chunks

    def consensus(at, before):
        return jnp.where(mask[pl.ds(at, 16), :] > 0.5, filled[pl.ds(at, 16), :], before)

    later_step(
        cost, wide, sums, last4,
        lambda at, before: 2.0 * consensus(at, before), third, field,
        lambda at: primal_in[pl.ds(at, 16), :],
    )

    def emit(source):
        def run(p, image):
            at = aligned(8 * p)
            old = source[pl.ds(at + PAD, 8), :]
            dual[pl.ds(at + PAD, 8), :] = jnp.maximum(
                old + 0.25 * (demand_n[pl.ds(at, 8), :] - image), 0.0
            )

        return run

    def chunk_body(c, state):
        wait_tiles(tiles_hbm, tiles, sems, chunks, c)
        pairs_a(tiles, cols4, field, (c * per_chunk, per_chunk), emit(dual_in), most)
        return state

    lax.fori_loop(0, chunks, chunk_body, 0)
    transpose_pass(tiles, order, order4, follows, dual, sums_next, most)

    def pull(at, before):
        start = primal_in[pl.ds(at, 16), :]
        middle = consensus(at, start)
        return before - (start - middle) + middle

    later_step(
        cost, wide, sums_next, last4, pull, primal_out, field,
        lambda at: third[pl.ds(at, 16), :],
    )
    weigh(primal_out, prob, node_of, root_blocks, node_blocks, group, total, vals, root_part, node_part)

    def rest_body(i, state):
        at = aligned(16 * i, 16)
        start = primal_in[pl.ds(at, 16), :]
        rest_out[pl.ds(at, 16), :] = (
            start - consensus(at, start) + primal_out[pl.ds(at, 16), :]
        )
        return state

    loop(rows // 16, 8, rest_body)
    pairs_a(tiles, cols4, field, (0, pairs), emit(dual), most)

    def order_body(r, state):
        dual_final[pl.ds(aligned(8 * r), 8), :] = pick_pair(
            dual, inverse4[2 * r], inverse4[2 * r + 1]
        )
        return state

    loop(pairs, 16, order_body)


def last_kernel(node_of, rest, root_mean, node_mean, root_row, node_row, multiplier, filled, mask):
    group = lax.axis_index("leaf")
    fill_means(root_mean, node_mean, root_row, node_row, node_of, group, filled, mask)

    def body(i, state):
        at = aligned(16 * i, 16)
        left = rest[pl.ds(at, 16), :] - filled[pl.ds(at, 16), :]
        multiplier[pl.ds(at, 16), :] = jnp.where(mask[pl.ds(at, 16), :] > 0.5, left, 0.0)
        return state

    loop(rest.shape[0] // 16, 8, body)


def wait_bytes(ref, sem):
    pltpu.make_async_copy(ref, ref, sem).wait()


def comm_kernel(
    ny, nx, nz, root_part, node_part, root_out, node_out,
    r0, n0, rsum, nsum, r1, n1, rz, r2, root_all, node_all, send, recv,
):
    sub, leaf = lax.axis_index("sub"), lax.axis_index("leaf")
    z, core = sub // 2, sub % 2
    y, x = leaf // nx, leaf % nx
    cells = ny * nx
    chunk = r1.shape[0] // max(cells - 1, 1)
    keep = chunk - 8
    rows = nsum.shape[0] // nz
    width = rows - 8
    half_r, half_n = cells * chunk, nz * rows

    partner = {"sub": z * 2 + (1 - core), "leaf": leaf}
    plane = []
    for k in range(1, cells):
        ky, kx = k // nx, k % nx
        other = ((y + ky) % ny) * nx + (x + kx) % nx
        plane.append((k, other, {"sub": sub, "leaf": other}))
    column = []
    for k in range(1, nz):
        other = (z + k) % nz
        column.append((k, other, {"sub": other * 2 + core, "leaf": leaf}))

    barrier = pltpu.get_barrier_semaphore()
    peers = [partner] + [p[2] for p in plane] + [p[2] for p in column]
    for peer in peers:
        pl.semaphore_signal(barrier, inc=1, device_id=peer, device_id_type=MESH)
    pl.semaphore_wait(barrier, len(peers))

    def push(src, dst, which, peer):
        pltpu.make_async_remote_copy(
            src_ref=src, dst_ref=dst, send_sem=send.at[which], recv_sem=recv.at[which],
            device_id=peer, device_id_type=MESH,
        ).start()

    push(node_part.at[pl.ds(aligned((1 - core) * half_n), half_n)], n0, 0, partner)
    push(root_part.at[pl.ds(aligned((1 - core) * half_r), half_r)], r0, 1, partner)
    wait_bytes(n0, recv.at[0])
    nsum[...] = node_part[pl.ds(aligned(core * half_n), half_n), :] + n0[...]
    for k, other, peer in column:
        push(
            nsum.at[pl.ds(aligned(other * rows), rows)],
            n1.at[pl.ds((k - 1) * rows, rows)], 2, peer,
        )
    wait_bytes(r0, recv.at[1])
    rsum[...] = root_part[pl.ds(aligned(core * half_r), half_r), :] + r0[...]
    for k, other, peer in plane:
        push(
            rsum.at[pl.ds(aligned(other * chunk), chunk)],
            r1.at[pl.ds((k - 1) * chunk, chunk)], 3, peer,
        )
    if nz > 1:
        wait_bytes(n1, recv.at[2])
    acc = nsum[pl.ds(aligned(z * rows), rows), :]
    for k in range(1, nz):
        acc = acc + n1[pl.ds((k - 1) * rows, rows), :]
    mine = (core * nz + z) * width
    node_all[pl.ds(aligned(mine), width), :] = acc[:width] / acc[width:width + 1]
    for k, other, peer in column:
        spot = node_all.at[pl.ds(aligned(mine), width)]
        push(spot, spot, 4, peer)
    if cells > 1:
        wait_bytes(r1, recv.at[3])
    acc = rsum[pl.ds(aligned(leaf * chunk), chunk), :]
    for k in range(1, cells):
        acc = acc + r1[pl.ds((k - 1) * chunk, chunk), :]
    rz[...] = acc
    for k, other, peer in column:
        push(rz, r2.at[pl.ds((k - 1) * chunk, chunk)], 5, peer)
    if nz > 1:
        wait_bytes(node_all.at[pl.ds(0, (nz - 1) * width)], recv.at[4])
    spot = node_all.at[pl.ds(aligned(core * nz * width), nz * width)]
    push(spot, spot, 6, partner)
    if nz > 1:
        wait_bytes(r2, recv.at[5])
    total = rz[...]
    for k in range(1, nz):
        total = total + r2[pl.ds((k - 1) * chunk, chunk), :]
    mine = (core * cells + leaf) * keep
    root_all[pl.ds(aligned(mine), keep), :] = total[:keep] / total[keep:keep + 1]
    for k, other, peer in plane:
        spot = root_all.at[pl.ds(aligned(mine), keep)]
        push(spot, spot, 7, peer)
    if cells > 1:
        wait_bytes(root_all.at[pl.ds(0, (cells - 1) * keep)], recv.at[7])
    spot = root_all.at[pl.ds(aligned(core * cells * keep), cells * keep)]
    push(spot, spot, 8, partner)
    wait_bytes(node_all.at[pl.ds(0, nz * width)], recv.at[6])
    node_out[...] = node_all[...]
    wait_bytes(root_all.at[pl.ds(0, cells * keep)], recv.at[8])
    root_out[...] = root_all[...]
    wait_bytes(n0, send.at[0])
    wait_bytes(r0, send.at[1])
    if nz > 1:
        wait_bytes(n1, send.at[2])
        wait_bytes(node_all.at[pl.ds(0, (nz - 1) * width)], send.at[4])
        wait_bytes(r2, send.at[5])
    if cells > 1:
        wait_bytes(r1, send.at[3])
        wait_bytes(root_all.at[pl.ds(0, (cells - 1) * keep)], send.at[7])
    wait_bytes(node_all.at[pl.ds(0, nz * width)], send.at[6])
    wait_bytes(root_all.at[pl.ds(0, cells * keep)], send.at[8])


def comm(root_part, node_part, root_count, width):
    leaf, sub = lax.axis_size("leaf"), lax.axis_size("sub")
    nz = sub // 2
    ny = 4 if leaf == 16 else 1
    nx = leaf // ny
    chunk = root_part.shape[0] // (2 * leaf)
    rows = width + 8
    vm = functools.partial(pltpu.VMEM, dtype=F32)
    return pl.pallas_call(
        functools.partial(comm_kernel, ny, nx, nz),
        out_shape=[
            jax.ShapeDtypeStruct((root_count, LANES), F32),
            jax.ShapeDtypeStruct((8 * width, LANES), F32),
        ],
        in_specs=[pl.BlockSpec(memory_space=pltpu.VMEM)] * 2,
        out_specs=[pl.BlockSpec(memory_space=pltpu.VMEM)] * 2,
        scratch_shapes=[
            vm((leaf * chunk, LANES)),
            vm((nz * rows, LANES)),
            vm((leaf * chunk, LANES)),
            vm((nz * rows, LANES)),
            vm(((leaf - 1) * chunk, LANES)),
            vm((max(nz - 1, 1) * rows, LANES)),
            vm((chunk, LANES)),
            vm((max(nz - 1, 1) * chunk, LANES)),
            vm((root_count, LANES)),
            vm((8 * width, LANES)),
            pltpu.SemaphoreType.DMA((9,)),
            pltpu.SemaphoreType.DMA((9,)),
        ],
        compiler_params=pltpu.CompilerParams(collective_id=0, has_side_effects=True),
        name="mean_exchange",
    )(root_part, node_part)


def as_rows(field):
    count, size = field.shape
    return field.reshape(count, size // LANES, LANES).transpose(1, 0, 2).reshape(-1, LANES)


def from_rows(rows):
    blocks = rows.shape[0] // 4
    return rows.reshape(blocks, 4, LANES).transpose(1, 0, 2).reshape(4, blocks * LANES)


def per_device(
    tiles, tile_rows, tile_cols, cost, demand, upper, prob, node_of_scen, root_blocks, node_blocks
):
    nt = tiles.shape[0]
    nvt = cost.shape[1] // LANES
    nct = demand.shape[1] // LANES
    width = node_blocks.shape[1]
    root_count = root_blocks.shape[0]
    leaf = lax.axis_size("leaf")
    chunks = 8
    most = 32
    with jax.named_scope("tables"):
        n = jnp.arange(nt, dtype=jnp.int32)
        ahead = (tile_cols[None, :] < tile_cols[:, None]) | (
            (tile_cols[None, :] == tile_cols[:, None]) & (n[None, :] < n[:, None])
        )
        rank = jnp.sum(ahead.astype(jnp.int32), axis=1)
        place = rank[None, :] == n[:, None]
        order = jnp.sum(jnp.where(place, n[None, :], 0), axis=1)
        sorted_col = jnp.sum(jnp.where(place, tile_cols[None, :], 0), axis=1)
        follows = jnp.concatenate(
            [jnp.zeros((1,), F32), (sorted_col[1:] == sorted_col[:-1]).astype(F32)]
        )
        v = jnp.arange(nvt, dtype=jnp.int32)
        upto = jnp.sum((tile_cols[None, :] <= v[:, None]).astype(jnp.int32), axis=1)
        has = jnp.sum((tile_cols[None, :] == v[:, None]).astype(jnp.int32), axis=1)
        last4 = 4 * jnp.where(has > 0, upto - 1, nt)
        inverse4 = 4 * jnp.sum(
            jnp.where(tile_rows[None, :] == jnp.arange(nct)[:, None], n[None, :], 0), axis=1
        )
        cols4, rows4, order4 = 4 * tile_cols, 4 * tile_rows, 4 * order
    cost_r, demand_r = as_rows(cost), as_rows(demand)
    upper_r = upper.reshape(nvt, LANES)
    root_row = root_blocks.reshape(1, root_count)
    part_rows = 2 * leaf * (root_count // (2 * leaf) + 8)
    sm = pl.BlockSpec(memory_space=pltpu.SMEM)
    vm = pl.BlockSpec(memory_space=pltpu.VMEM)
    hbm = pl.BlockSpec(memory_space=pl.ANY)
    shape = jax.ShapeDtypeStruct
    params = pltpu.CompilerParams(vmem_limit_bytes=62 * 1024 * 1024)
    pad_rows = PAD + 4 * nt + 16
    state_rows = 4 * nvt
    primal2, dual2, sums2, demand_n, wide, root_part, node_part = pl.pallas_call(
        functools.partial(first_kernel, chunks, most),
        out_shape=[
            shape((state_rows, LANES), F32),
            shape((pad_rows, LANES), F32),
            shape((pad_rows, LANES), F32),
            shape((4 * nt, LANES), F32),
            shape((state_rows, LANES), F32),
            shape((part_rows, LANES), F32),
            shape((8 * (width + 8), LANES), F32),
        ],
        in_specs=[sm] * 10 + [hbm, vm, vm, vm],
        out_specs=[vm] * 7,
        scratch_shapes=[
            pltpu.VMEM(tiles.shape, BF16),
            pltpu.VMEM((state_rows + 2 * PAD, LANES), F32),
            pltpu.VMEM((nvt, LANES), F32),
            pltpu.VMEM((4 * width, LANES), F32),
            pltpu.VMEM((4 * nct + 2 * PAD, LANES), F32),
            pltpu.SemaphoreType.DMA((chunks,)),
        ],
        compiler_params=params,
        name="first_iteration",
    )(
        cols4, rows4, order, order4, follows, last4, prob, node_of_scen, root_blocks, node_blocks,
        tiles, cost_r, demand_r, upper_r,
    )
    root_mean, node_mean = comm(root_part, node_part, root_count, width)
    primal, dual, rest, root_part, node_part = pl.pallas_call(
        functools.partial(second_kernel, chunks, most),
        out_shape=[
            shape((state_rows, LANES), F32),
            shape((4 * nct, LANES), F32),
            shape((state_rows, LANES), F32),
            shape((part_rows, LANES), F32),
            shape((8 * (width + 8), LANES), F32),
        ],
        in_specs=[sm] * 10 + [hbm] + [vm] * 10,
        out_specs=[vm] * 5,
        scratch_shapes=[
            pltpu.VMEM(tiles.shape, BF16),
            pltpu.VMEM((state_rows + 2 * PAD, LANES), F32),
            pltpu.VMEM((nvt, LANES), F32),
            pltpu.VMEM((4 * width, LANES), F32),
            pltpu.VMEM((pad_rows, LANES), F32),
            pltpu.VMEM((pad_rows, LANES), F32),
            pltpu.VMEM((state_rows, LANES), F32),
            pltpu.VMEM((state_rows, LANES), F32),
            pltpu.VMEM((state_rows, LANES), F32),
            pltpu.SemaphoreType.DMA((chunks,)),
        ],
        compiler_params=params,
        name="second_iteration",
    )(
        cols4, order, order4, follows, last4, inverse4, prob, node_of_scen, root_blocks, node_blocks,
        tiles, cost_r, wide, demand_n, primal2, dual2, sums2, root_mean, node_mean, root_row, node_blocks,
    )
    root_mean, node_mean = comm(root_part, node_part, root_count, width)
    multiplier = pl.pallas_call(
        last_kernel,
        out_shape=shape((state_rows, LANES), F32),
        in_specs=[sm] + [vm] * 5,
        out_specs=vm,
        scratch_shapes=[
            pltpu.VMEM((state_rows, LANES), F32),
            pltpu.VMEM((state_rows, LANES), F32),
        ],
        compiler_params=params,
        name="multiplier_update",
    )(node_of_scen, rest, root_mean, node_mean, root_row, node_blocks)
    return from_rows(primal), from_rows(dual), from_rows(multiplier)


def solution(mesh):
    split = P(("sub", "leaf"), None)
    return jax.shard_map(
        per_device,
        mesh=mesh,
        in_specs=(
            P(), P(), P(), split, split, P(), P(("sub", "leaf")), P(("sub", "leaf")), P(), P(),
        ),
        out_specs=(split, split, split),
        check_vma=False,
    )
```

```python
import functools

import jax
import jax.numpy as jnp
from jax import lax
from jax.experimental import pallas as pl
from jax.experimental.pallas import tpu as pltpu
from jax.sharding import PartitionSpec as P

F32 = jnp.float32
BF16 = jnp.bfloat16
MESH = pl.DeviceIdType.MESH
LANES = 128
PAD = 8


def aligned(value, step=8):
    return pl.multiple_of(value, step)


def top_rows():
    return lax.broadcasted_iota(jnp.int32, (8, LANES), 0) < 4


def unroll_of(count, most):
    step = min(count, most)
    while count % step:
        step -= 1
    return step


def loop(count, most, body, carry=0, first=0):
    step = unroll_of(count, most)

    def outer(i, state):
        base = first + i * step
        return lax.fori_loop(0, step, lambda u, inner: body(base + u, inner), state, unroll=True)

    return lax.fori_loop(0, count // step, outer, carry)


def start_tiles(tiles_hbm, tiles, sems, chunks):
    size = tiles.shape[0] // chunks
    for c in range(chunks):
        part = pl.ds(c * size, size)
        pltpu.make_async_copy(tiles_hbm.at[part], tiles.at[part], sems.at[c]).start()


def wait_tiles(tiles_hbm, tiles, sems, chunks, c):
    size = tiles.shape[0] // chunks
    part = pl.ds(c * size, size)
    pltpu.make_async_copy(tiles_hbm.at[part], tiles.at[part], sems.at[c]).wait()


def pick_pair(ref, first4, second4):
    low = ref[pl.ds(first4 + PAD, 8), :]
    high = ref[pl.ds(second4 + (PAD - 4), 8), :]
    return jnp.where(top_rows(), low, high)


def spread_upper(upper, wide):
    blocks = upper.shape[0]
    for s in range(4):
        wide[pl.ds(s, blocks, stride=4), :] = upper[...]


def pairs_a(tiles, cols4, field, pairs, emit, most):
    def body(p, state):
        lhs = pick_pair(field, cols4[2 * p], cols4[2 * p + 1]).astype(BF16)
        rhs = tiles[pl.ds(2 * p, 2)].reshape(2 * LANES, LANES)
        both = lax.dot_general(lhs, rhs, (((1,), (1,)), ((), ())), preferred_element_type=F32)
        emit(p, jnp.where(top_rows(), both[:, :LANES], both[:, LANES:]))
        return state

    first, count = pairs
    loop(count, most, body, 0, first)


def transpose_pass(tiles, order, order4, follows, dual, sums, pairs, carry, most):
    def body(p, carry):
        a, b = 2 * p, 2 * p + 1
        top = top_rows()
        low = dual[pl.ds(order4[a] + PAD, 8), :]
        high = dual[pl.ds(order4[b] + (PAD - 4), 8), :]
        lhs = jnp.concatenate([jnp.where(top, low, 0.0), jnp.where(top, 0.0, high)], axis=1)
        rhs = jnp.concatenate([tiles[order[a]], tiles[order[b]]], axis=0)
        own = lax.dot_general(
            lhs.astype(BF16), rhs, (((1,), (0,)), ((), ())), preferred_element_type=F32
        )
        fa, fb = follows[a], follows[b]
        other = pltpu.roll(own, 4, 0)
        within = own + jnp.where(top, 0.0, fb) * other
        full = jnp.where(top, fb * own + other, within)
        both = fa * fb
        sums[pl.ds(aligned(PAD + 8 * p), 8), :] = within + jnp.where(top, fa, both) * carry
        return both * carry + full

    first, count = pairs
    return loop(count, most, body, carry, first)


def first_step(cost, wide, field):
    rows = cost.shape[0]

    def body(i, state):
        at = aligned(16 * i, 16)
        moved = -cost[pl.ds(at, 16), :].astype(F32) * 0.5
        field[pl.ds(at + PAD, 16), :] = 2.0 * jnp.clip(moved, 0.0, wide[pl.ds(at, 16), :])
        return state

    loop(rows // 16, 8, body)


def later_step(cost, wide, sums, last4, base, primal_out, field, old):
    rows = cost.shape[0]

    def body(i, state):
        at = aligned(16 * i, 16)
        gradient = jnp.concatenate(
            [
                pick_pair(sums, last4[4 * i], last4[4 * i + 1]),
                pick_pair(sums, last4[4 * i + 2], last4[4 * i + 3]),
            ],
            axis=0,
        )
        before = old(at)
        moved = base(at, before) - cost[pl.ds(at, 16), :].astype(F32) + gradient
        after = jnp.clip(moved * 0.5, 0.0, wide[pl.ds(at, 16), :])
        primal_out[pl.ds(at, 16), :] = after
        field[pl.ds(at + PAD, 16), :] = 2.0 * after - before
        return state

    loop(rows // 16, 8, body)


def weigh_root(primal, prob, root_blocks, total, root_part):
    blocks = total.shape[0]
    acc = prob[0] * primal[pl.ds(0, blocks, stride=4), :]
    for s in range(1, 4):
        acc = acc + prob[s] * primal[pl.ds(s, blocks, stride=4), :]
    total[...] = acc
    root_count = root_blocks.shape[0]
    pieces = (root_part.shape[0] - root_count) // 8
    each = root_count // pieces
    split = each + 8
    weight = jnp.full((8, LANES), prob[0] + prob[1] + prob[2] + prob[3], F32)

    def body(i, state):
        for u in range(each):
            root_part[pl.ds(i * split + u, 1), :] = total[pl.ds(root_blocks[i * each + u], 1), :]
        root_part[pl.ds(aligned(i * split + each), 8), :] = weight
        return state

    lax.fori_loop(0, pieces, body, 0)


def weigh_nodes(primal, prob, node_of, local_of, node_blocks, vals, node_part):
    width = node_part.shape[0] // 8 - 8
    for s in range(4):
        base = node_of[s] * width

        def body(b, state):
            row = primal[pl.ds(4 * node_blocks[base + b] + s, 1), :]
            vals[pl.ds(s * width + b, 1), :] = row
            return state

        loop(width, 16, body)
    for m in range(8):
        slot = m
        share = []
        for s in range(4):
            gap = local_of[s] - m
            share.append(prob[s] * (1 - jnp.minimum(gap * gap, 1)).astype(F32))
        part = share[0] * vals[pl.ds(0, width), :]
        for s in range(1, 4):
            part = part + share[s] * vals[pl.ds(s * width, width), :]
        node_part[pl.ds(slot * (width + 8), width), :] = part
        node_part[pl.ds(slot * (width + 8) + width, 8), :] = jnp.full(
            (8, LANES), share[0] + share[1] + share[2] + share[3], F32
        )


def split_two(value):
    high = value.astype(BF16)
    low = (value - high.astype(F32)).astype(BF16)
    return jnp.concatenate([high, low], axis=1)


def mark_blocks(root_row, node_row, node_of, hot_root, hot_node, mask):
    blocks = hot_root.shape[0]
    chunk = min(blocks, 128)
    width = hot_node.shape[1]
    count = hot_root.shape[1]
    ones_root = jnp.ones((count, LANES), BF16)
    ones_node = jnp.ones((width, LANES), BF16)

    def body(i, state):
        at = aligned(i * chunk, chunk)
        here = lax.broadcasted_iota(jnp.int32, (chunk, count), 0) + at
        hot = (here == root_row[...]).astype(F32).astype(BF16)
        hot_root[pl.ds(at, chunk), :] = hot
        root_mask = jnp.dot(hot, ones_root, preferred_element_type=F32)
        here = lax.broadcasted_iota(jnp.int32, (chunk, width), 0) + at
        for s in range(4):
            hot = (here == node_row[pl.ds(node_of[s], 1), :]).astype(F32).astype(BF16)
            hot_node[pl.ds(aligned(s * blocks + at, chunk), chunk), :] = hot
            mask[pl.ds(4 * at + s, chunk, stride=4), :] = root_mask + jnp.dot(
                hot, ones_node, preferred_element_type=F32
            )
        return state

    lax.fori_loop(0, blocks // chunk, body, 0)


def fill_means(root_mean, node_mean, hot_root, hot_node, local_of, filled):
    blocks = hot_root.shape[0]
    chunk = min(blocks, 128)
    width = node_mean.shape[0] // 8
    root_rhs = split_two(root_mean[...])
    node_rhs = []
    for s in range(4):
        start = local_of[s] * width
        node_rhs.append(split_two(node_mean[pl.ds(start, width), :]))

    def body(i, state):
        at = aligned(i * chunk, chunk)
        got = jnp.dot(hot_root[pl.ds(at, chunk), :], root_rhs, preferred_element_type=F32)
        root_fill = got[:, :LANES] + got[:, LANES:]
        for s in range(4):
            hot = hot_node[pl.ds(aligned(s * blocks + at, chunk), chunk), :]
            got = jnp.dot(hot, node_rhs[s], preferred_element_type=F32)
            filled[pl.ds(4 * at + s, chunk, stride=4), :] = (
                root_fill + got[:, :LANES] + got[:, LANES:]
            )
        return state

    lax.fori_loop(0, blocks // chunk, body, 0)


def wait_bytes(ref, sem):
    pltpu.make_async_copy(ref, ref, sem).wait()


class Exchange:
    def __init__(self, ny, nx, nz, bufs, send, recv):
        (self.root_part, self.node_part, self.r0, self.n0, self.rsum, self.nsum, self.r1, self.n1,
         self.rz, self.r2, self.root_all, self.node_all) = bufs
        self.send, self.recv = send, recv
        sub, leaf = lax.axis_index("sub"), lax.axis_index("leaf")
        z, core = sub // 2, sub % 2
        y, x = leaf // nx, leaf % nx
        self.z, self.core, self.leaf, self.nz = z, core, leaf, nz
        self.cells = ny * nx
        self.chunk = self.rsum.shape[0] // self.cells
        self.rows = self.nsum.shape[0] // nz
        self.partner = {"sub": z * 2 + (1 - core), "leaf": leaf}
        self.plane, self.column = [], []
        for k in range(1, self.cells):
            other = ((y + k // nx) % ny) * nx + (x + k % nx) % nx
            self.plane.append((k, other, {"sub": sub, "leaf": other}))
        for k in range(1, nz):
            other = (z + k) % nz
            self.column.append((k, other, {"sub": other * 2 + core, "leaf": leaf}))
        self.peers = [self.partner] + [p[2] for p in self.plane] + [p[2] for p in self.column]

    def push(self, src, dst, which, peer):
        pltpu.make_async_remote_copy(
            src_ref=src, dst_ref=dst, send_sem=self.send.at[which], recv_sem=self.recv.at[which],
            device_id=peer, device_id_type=MESH,
        ).start()

    def root_to_partner(self):
        half = self.cells * self.chunk
        src = self.root_part.at[pl.ds(aligned((1 - self.core) * half), half)]
        self.push(src, self.r0, 1, self.partner)

    def node_to_partner(self):
        half = self.nz * self.rows
        src = self.node_part.at[pl.ds(aligned((1 - self.core) * half), half)]
        self.push(src, self.n0, 0, self.partner)

    def root_to_plane(self):
        half = self.cells * self.chunk
        wait_bytes(self.r0, self.recv.at[1])
        self.rsum[...] = self.root_part[pl.ds(aligned(self.core * half), half), :] + self.r0[...]
        for k, other, peer in self.plane:
            self.push(
                self.rsum.at[pl.ds(aligned(other * self.chunk), self.chunk)],
                self.r1.at[pl.ds((k - 1) * self.chunk, self.chunk)], 3, peer,
            )

    def node_to_column(self):
        half = self.nz * self.rows
        wait_bytes(self.n0, self.recv.at[0])
        self.nsum[...] = self.node_part[pl.ds(aligned(self.core * half), half), :] + self.n0[...]
        for k, other, peer in self.column:
            self.push(
                self.nsum.at[pl.ds(aligned(other * self.rows), self.rows)],
                self.n1.at[pl.ds((k - 1) * self.rows, self.rows)], 2, peer,
            )

    def node_back(self):
        width = self.rows - 8
        wait_bytes(self.n1, self.recv.at[2])
        acc = self.nsum[pl.ds(aligned(self.z * self.rows), self.rows), :]
        for k in range(1, self.nz):
            acc = acc + self.n1[pl.ds((k - 1) * self.rows, self.rows), :]
        spot = pl.ds(aligned((self.core * self.nz + self.z) * width), width)
        self.node_all[spot, :] = acc[:width] / acc[width:width + 1]
        for k, other, peer in self.column:
            self.push(self.node_all.at[spot], self.node_all.at[spot], 4, peer)

    def root_to_column(self):
        wait_bytes(self.r1, self.recv.at[3])
        acc = self.rsum[pl.ds(aligned(self.leaf * self.chunk), self.chunk), :]
        for k in range(1, self.cells):
            acc = acc + self.r1[pl.ds((k - 1) * self.chunk, self.chunk), :]
        self.rz[...] = acc
        for k, other, peer in self.column:
            self.push(self.rz, self.r2.at[pl.ds((k - 1) * self.chunk, self.chunk)], 5, peer)

    def root_back(self):
        keep = self.chunk - 8
        wait_bytes(self.r2, self.recv.at[5])
        total = self.rz[...]
        for k in range(1, self.nz):
            total = total + self.r2[pl.ds((k - 1) * self.chunk, self.chunk), :]
        spot = pl.ds(aligned((self.core * self.cells + self.leaf) * keep), keep)
        self.root_all[spot, :] = total[:keep] / total[keep:keep + 1]
        for k, other, peer in self.plane:
            self.push(self.root_all.at[spot], self.root_all.at[spot], 7, peer)

    def node_home(self):
        half = self.nz * (self.rows - 8)
        wait_bytes(self.node_all.at[pl.ds(0, half - (self.rows - 8))], self.recv.at[4])
        spot = self.node_all.at[pl.ds(aligned(self.core * half), half)]
        self.push(spot, spot, 6, self.partner)

    def root_home(self):
        keep = self.chunk - 8
        half = self.cells * keep
        wait_bytes(self.root_all.at[pl.ds(0, half - keep)], self.recv.at[7])
        spot = self.root_all.at[pl.ds(aligned(self.core * half), half)]
        self.push(spot, spot, 8, self.partner)

    def finish(self):
        wait_bytes(self.node_all.at[pl.ds(0, self.nz * (self.rows - 8))], self.recv.at[6])
        wait_bytes(self.root_all.at[pl.ds(0, self.cells * (self.chunk - 8))], self.recv.at[8])

    def drain(self):
        width, keep = self.rows - 8, self.chunk - 8
        sent = [
            self.n0, self.r0, self.n1, self.r1,
            self.node_all.at[pl.ds(0, (self.nz - 1) * width)],
            self.r2,
            self.node_all.at[pl.ds(0, self.nz * width)],
            self.root_all.at[pl.ds(0, (self.cells - 1) * keep)],
            self.root_all.at[pl.ds(0, self.cells * keep)],
        ]
        for which, ref in enumerate(sent):
            wait_bytes(ref, self.send.at[which])


def whole_kernel(
    chunks, most, ny, nx, nz,
    cols4, rows4, order, order4, follows, last4, inverse4, prob, node_of, local_of, root_blocks, node_blocks,
    tiles_hbm, cost, demand, upper, root_row, node_row,
    primal_hbm, dual_hbm, multiplier_hbm,
    tiles, field, wide, demand_f, demand_n, dual, sums, second, third, last, filled, mask, rest,
    dual_rows, total, vals, hot_root, hot_node, *others,
):
    bufs, (sems, out_sems, send0, recv0, send1, recv1) = others[:24], others[24:]
    rounds = [
        Exchange(ny, nx, nz, bufs[:12], send0, recv0),
        Exchange(ny, nx, nz, bufs[12:], send1, recv1),
    ]
    start_tiles(tiles_hbm, tiles, sems, chunks)
    barrier = pltpu.get_barrier_semaphore()
    for peer in rounds[0].peers:
        pl.semaphore_signal(barrier, inc=1, device_id=peer, device_id_type=MESH)
    pairs = tiles.shape[0] // 2
    per_chunk = pairs // chunks
    rows = cost.shape[0]
    zero = jnp.zeros((8, LANES), F32)
    sums[pl.ds(PAD + 8 * pairs, 8), :] = zero

    spread_upper(upper, wide)
    demand_f[pl.ds(PAD, demand.shape[0]), :] = demand[...].astype(F32)
    first_step(cost, wide, field)

    def emit_first(p, image):
        want = pick_pair(demand_f, rows4[2 * p], rows4[2 * p + 1])
        demand_n[pl.ds(aligned(8 * p), 8), :] = want
        dual[pl.ds(aligned(PAD + 8 * p), 8), :] = jnp.maximum(0.25 * (want - image), 0.0)

    def emit_next(p, image):
        at = aligned(8 * p)
        old = dual[pl.ds(aligned(at + PAD), 8), :]
        dual[pl.ds(aligned(at + PAD), 8), :] = jnp.maximum(
            old + 0.25 * (demand_n[pl.ds(at, 8), :] - image), 0.0
        )

    def chunk_body(c, state):
        wait_tiles(tiles_hbm, tiles, sems, chunks, c)
        pairs_a(tiles, cols4, field, (c * per_chunk, per_chunk), emit_first, most)
        return state

    def forward(part):
        first, stop = part[0] * pairs // 8, part[1] * pairs // 8
        pairs_a(tiles, cols4, field, (first, stop - first), emit_next, most)

    def backward(part, carry):
        first, stop = part[0] * pairs // 8, part[1] * pairs // 8
        return transpose_pass(
            tiles, order, order4, follows, dual, sums, (first, stop - first), carry, most
        )

    lax.fori_loop(0, chunks, chunk_body, 0)
    backward((0, 8), zero)
    later_step(
        cost, wide, sums, last4, lambda at, before: before, second, field,
        lambda at: 0.5 * field[pl.ds(at + PAD, 16), :],
    )

    go = rounds[0]
    weigh_root(second, prob, root_blocks, total, go.root_part)
    pl.semaphore_wait(barrier, len(go.peers))
    go.root_to_partner()
    weigh_nodes(second, prob, node_of, local_of, node_blocks, vals, go.node_part)
    go.node_to_partner()
    go.root_to_plane()
    forward((0, 2))
    go.node_to_column()
    forward((2, 8))
    go.root_to_column()
    carry = backward((0, 2), zero)
    go.node_back()
    carry = backward((2, 6), carry)
    go.root_back()
    carry = backward((6, 8), carry)
    mark_blocks(root_row, node_row, node_of, hot_root, hot_node, mask)
    go.node_home()
    go.root_home()
    go.finish()
    fill_means(go.root_all, go.node_all, hot_root, hot_node, local_of, filled)

    def consensus(at, before):
        return jnp.where(mask[pl.ds(at, 16), :] > 0.5, filled[pl.ds(at, 16), :], before)

    later_step(
        cost, wide, sums, last4, lambda at, before: 2.0 * consensus(at, before), third, field,
        lambda at: second[pl.ds(at, 16), :],
    )
    forward((0, 8))
    backward((0, 8), zero)

    def pull(at, before):
        start = second[pl.ds(at, 16), :]
        middle = consensus(at, start)
        return before - (start - middle) + middle

    later_step(
        cost, wide, sums, last4, pull, last, field, lambda at: third[pl.ds(at, 16), :],
    )
    primal_copy = pltpu.make_async_copy(last, primal_hbm, out_sems.at[0])
    primal_copy.start()

    go = rounds[1]
    weigh_root(last, prob, root_blocks, total, go.root_part)
    go.root_to_partner()
    weigh_nodes(last, prob, node_of, local_of, node_blocks, vals, go.node_part)
    go.node_to_partner()
    go.root_to_plane()
    forward((0, 2))
    go.node_to_column()
    forward((2, 8))
    go.root_to_column()

    def order_body(r, state):
        dual_rows[pl.ds(aligned(8 * r), 8), :] = pick_pair(
            dual, inverse4[2 * r], inverse4[2 * r + 1]
        )
        return state

    loop(pairs, 16, order_body)
    dual_copy = pltpu.make_async_copy(dual_rows, dual_hbm, out_sems.at[1])
    dual_copy.start()
    go.node_back()

    def rest_body(i, state):
        at = aligned(16 * i, 16)
        start = second[pl.ds(at, 16), :]
        rest[pl.ds(at, 16), :] = start - consensus(at, start) + last[pl.ds(at, 16), :]
        return state

    loop(rows // 16, 8, rest_body)
    go.root_back()
    go.node_home()
    go.root_home()
    go.finish()
    fill_means(go.root_all, go.node_all, hot_root, hot_node, local_of, filled)

    def final_body(i, state):
        at = aligned(16 * i, 16)
        left = rest[pl.ds(at, 16), :] - filled[pl.ds(at, 16), :]
        third[pl.ds(at, 16), :] = jnp.where(mask[pl.ds(at, 16), :] > 0.5, left, 0.0)
        return state

    loop(rows // 16, 8, final_body)
    multiplier_copy = pltpu.make_async_copy(third, multiplier_hbm, out_sems.at[2])
    multiplier_copy.start()
    primal_copy.wait()
    dual_copy.wait()
    rounds[0].drain()
    rounds[1].drain()
    multiplier_copy.wait()


def as_rows(field):
    count, size = field.shape
    return field.reshape(count, size // LANES, LANES).transpose(1, 0, 2).reshape(-1, LANES)


def from_rows(rows):
    blocks = rows.shape[0] // 4
    return rows.reshape(blocks, 4, LANES).transpose(1, 0, 2).reshape(4, blocks * LANES)


def per_device(
    tiles, tile_rows, tile_cols, cost, demand, upper, prob, node_of_scen, root_blocks, node_blocks
):
    nt = tiles.shape[0]
    nvt = cost.shape[1] // LANES
    nct = demand.shape[1] // LANES
    width = node_blocks.shape[1]
    root_count = root_blocks.shape[0]
    leaf = lax.axis_size("leaf")
    chunks = 8
    most = 32
    with jax.named_scope("tables"):
        n = jnp.arange(nt, dtype=jnp.int32)
        ahead = (tile_cols[None, :] < tile_cols[:, None]) | (
            (tile_cols[None, :] == tile_cols[:, None]) & (n[None, :] < n[:, None])
        )
        rank = jnp.sum(ahead.astype(jnp.int32), axis=1)
        place = rank[None, :] == n[:, None]
        order = jnp.sum(jnp.where(place, n[None, :], 0), axis=1)
        sorted_col = jnp.sum(jnp.where(place, tile_cols[None, :], 0), axis=1)
        follows = jnp.concatenate(
            [jnp.zeros((1,), F32), (sorted_col[1:] == sorted_col[:-1]).astype(F32)]
        )
        v = jnp.arange(nvt, dtype=jnp.int32)
        upto = jnp.sum((tile_cols[None, :] <= v[:, None]).astype(jnp.int32), axis=1)
        has = jnp.sum((tile_cols[None, :] == v[:, None]).astype(jnp.int32), axis=1)
        last4 = 4 * jnp.where(has > 0, upto - 1, nt)
        inverse4 = 4 * jnp.sum(
            jnp.where(tile_rows[None, :] == jnp.arange(nct)[:, None], n[None, :], 0), axis=1
        )
        cols4, rows4, order4 = 4 * tile_cols, 4 * tile_rows, 4 * order
    local_of = node_of_scen - 8 * lax.axis_index("leaf")
    cost_r, demand_r = as_rows(cost), as_rows(demand)
    upper_r = upper.reshape(nvt, LANES)
    root_row = root_blocks.reshape(1, root_count)
    sub = lax.axis_size("sub")
    nz = sub // 2
    ny = 4 if leaf == 16 else 1
    nx = leaf // ny
    chunk = root_count // (2 * leaf) + 8
    node_rows = width + 8
    pad_rows = PAD + 4 * nt + 16
    state_rows = 4 * nvt
    sm = pl.BlockSpec(memory_space=pltpu.SMEM)
    vm = pl.BlockSpec(memory_space=pltpu.VMEM)
    hbm = pl.BlockSpec(memory_space=pl.ANY)

    def lines(count):
        return pltpu.VMEM((count, LANES), F32)

    exchange = [
        lines(2 * leaf * chunk),
        lines(8 * node_rows),
        lines(leaf * chunk),
        lines(nz * node_rows),
        lines(leaf * chunk),
        lines(nz * node_rows),
        lines((leaf - 1) * chunk),
        lines((nz - 1) * node_rows),
        lines(chunk),
        lines((nz - 1) * chunk),
        lines(root_count),
        lines(8 * width),
    ]
    primal, dual, multiplier = pl.pallas_call(
        functools.partial(whole_kernel, chunks, most, ny, nx, nz),
        out_shape=[
            jax.ShapeDtypeStruct((state_rows, LANES), F32),
            jax.ShapeDtypeStruct((4 * nct, LANES), F32),
            jax.ShapeDtypeStruct((state_rows, LANES), F32),
        ],
        in_specs=[sm] * 12 + [hbm] + [vm] * 5,
        out_specs=[hbm] * 3,
        scratch_shapes=[
            pltpu.VMEM(tiles.shape, BF16),
            lines(state_rows + 2 * PAD),
            lines(state_rows),
            lines(4 * nct + 2 * PAD),
            lines(4 * nt),
            lines(pad_rows),
            lines(pad_rows),
            lines(state_rows),
            lines(state_rows),
            lines(state_rows),
            lines(state_rows),
            lines(state_rows),
            lines(state_rows),
            lines(4 * nct),
            lines(nvt),
            lines(4 * width),
            pltpu.VMEM((nvt, root_count), BF16),
            pltpu.VMEM((4 * nvt, width), BF16),
            *exchange,
            *exchange,
            pltpu.SemaphoreType.DMA((chunks,)),
            pltpu.SemaphoreType.DMA((3,)),
            *[pltpu.SemaphoreType.DMA((9,))] * 4,
        ],
        compiler_params=pltpu.CompilerParams(
            collective_id=0, has_side_effects=True, vmem_limit_bytes=62 * 1024 * 1024
        ),
        name="hedging",
    )(
        cols4, rows4, order, order4, follows, last4, inverse4, prob, node_of_scen, local_of,
        root_blocks, node_blocks.reshape(-1), tiles, cost_r, demand_r, upper_r, root_row, node_blocks,
    )
    return from_rows(primal), from_rows(dual), from_rows(multiplier)


def solution(mesh):
    split = P(("sub", "leaf"), None)
    return jax.shard_map(
        per_device,
        mesh=mesh,
        in_specs=(
            P(), P(), P(), split, split, P(), P(("sub", "leaf")), P(("sub", "leaf")), P(), P(),
        ),
        out_specs=(split, split, split),
        check_vma=False,
    )
```

```python
import functools

import jax
import jax.numpy as jnp
from jax import lax
from jax.experimental import pallas as pl
from jax.experimental.pallas import tpu as pltpu
from jax.sharding import PartitionSpec as P

F32 = jnp.float32
BF16 = jnp.bfloat16
MESH = pl.DeviceIdType.MESH
LANES = 128
PAD = 8


def aligned(value, step=8):
    return pl.multiple_of(value, step)


def top_rows():
    return lax.broadcasted_iota(jnp.int32, (8, LANES), 0) < 4


def unroll_of(count, most):
    step = min(count, most)
    while count % step:
        step -= 1
    return step


def loop(count, most, body, carry=0, first=0):
    step = unroll_of(count, most)

    def outer(i, state):
        base = first + i * step
        return lax.fori_loop(0, step, lambda u, inner: body(base + u, inner), state, unroll=True)

    return lax.fori_loop(0, count // step, outer, carry)


def start_tiles(tiles_hbm, tiles, sems, chunks):
    size = tiles.shape[0] // chunks
    for c in range(chunks):
        part = pl.ds(c * size, size)
        pltpu.make_async_copy(tiles_hbm.at[part], tiles.at[part], sems.at[c]).start()


def wait_tiles(tiles_hbm, tiles, sems, chunks, c):
    size = tiles.shape[0] // chunks
    part = pl.ds(c * size, size)
    pltpu.make_async_copy(tiles_hbm.at[part], tiles.at[part], sems.at[c]).wait()


def pick_pair(ref, first4, second4):
    low = ref[pl.ds(first4 + PAD, 8), :]
    high = ref[pl.ds(second4 + (PAD - 4), 8), :]
    return jnp.where(top_rows(), low, high)


def spread_upper(upper, wide):
    blocks = upper.shape[0]
    for s in range(4):
        wide[pl.ds(s, blocks, stride=4), :] = upper[...]


def pairs_a(tiles, cols4, field, pairs, emit, most):
    def body(p, state):
        lhs = pick_pair(field, cols4[2 * p], cols4[2 * p + 1]).astype(BF16)
        rhs = tiles[pl.ds(2 * p, 2)].reshape(2 * LANES, LANES)
        both = lax.dot_general(lhs, rhs, (((1,), (1,)), ((), ())), preferred_element_type=F32)
        emit(p, jnp.where(top_rows(), both[:, :LANES], both[:, LANES:]))
        return state

    first, count = pairs
    loop(count, most, body, 0, first)


def transpose_pass(tiles, order, order4, follows, dual, sums, pairs, carry, most):
    def body(p, carry):
        a, b = 2 * p, 2 * p + 1
        top = top_rows()
        low = dual[pl.ds(order4[a] + PAD, 8), :]
        high = dual[pl.ds(order4[b] + (PAD - 4), 8), :]
        lhs = jnp.concatenate([jnp.where(top, low, 0.0), jnp.where(top, 0.0, high)], axis=1)
        rhs = jnp.concatenate([tiles[order[a]], tiles[order[b]]], axis=0)
        own = lax.dot_general(
            lhs.astype(BF16), rhs, (((1,), (0,)), ((), ())), preferred_element_type=F32
        )
        fa, fb = follows[a], follows[b]
        other = pltpu.roll(own, 4, 0)
        within = own + jnp.where(top, 0.0, fb) * other
        full = jnp.where(top, fb * own + other, within)
        both = fa * fb
        sums[pl.ds(aligned(PAD + 8 * p), 8), :] = within + jnp.where(top, fa, both) * carry
        return both * carry + full

    first, count = pairs
    return loop(count, most, body, carry, first)


def first_step(cost, wide, field):
    rows = cost.shape[0]

    def body(i, state):
        at = aligned(16 * i, 16)
        moved = -cost[pl.ds(at, 16), :].astype(F32) * 0.5
        field[pl.ds(at + PAD, 16), :] = 2.0 * jnp.clip(moved, 0.0, wide[pl.ds(at, 16), :])
        return state

    loop(rows // 16, 8, body)


def later_step(cost, wide, sums, last4, base, primal_out, field, old):
    rows = cost.shape[0]

    def body(i, state):
        at = aligned(16 * i, 16)
        gradient = jnp.concatenate(
            [
                pick_pair(sums, last4[4 * i], last4[4 * i + 1]),
                pick_pair(sums, last4[4 * i + 2], last4[4 * i + 3]),
            ],
            axis=0,
        )
        before = old(at)
        moved = base(at, before) - cost[pl.ds(at, 16), :].astype(F32) + gradient
        after = jnp.clip(moved * 0.5, 0.0, wide[pl.ds(at, 16), :])
        primal_out[pl.ds(at, 16), :] = after
        field[pl.ds(at + PAD, 16), :] = 2.0 * after - before
        return state

    loop(rows // 16, 8, body)


def weigh_root(primal, prob, root_blocks, total, root_part):
    blocks = total.shape[0]
    acc = prob[0] * primal[pl.ds(0, blocks, stride=4), :]
    for s in range(1, 4):
        acc = acc + prob[s] * primal[pl.ds(s, blocks, stride=4), :]
    total[...] = acc
    root_count = root_blocks.shape[0]
    pieces = (root_part.shape[0] - root_count) // 8
    each = root_count // pieces
    split = each + 8
    weight = jnp.full((8, LANES), prob[0] + prob[1] + prob[2] + prob[3], F32)

    def body(i, state):
        for u in range(each):
            root_part[pl.ds(i * split + u, 1), :] = total[pl.ds(root_blocks[i * each + u], 1), :]
        root_part[pl.ds(aligned(i * split + each), 8), :] = weight
        return state

    lax.fori_loop(0, pieces, body, 0)


def weigh_nodes(primal, prob, node_of, local_of, node_blocks, vals, node_part):
    width = node_part.shape[0] // 8 - 8
    for s in range(4):
        base = node_of[s] * width

        def body(b, state):
            row = primal[pl.ds(4 * node_blocks[base + b] + s, 1), :]
            vals[pl.ds(s * width + b, 1), :] = row
            return state

        loop(width, 16, body)
    for m in range(8):
        slot = m
        share = []
        for s in range(4):
            gap = local_of[s] - m
            share.append(prob[s] * (1 - jnp.minimum(gap * gap, 1)).astype(F32))
        part = share[0] * vals[pl.ds(0, width), :]
        for s in range(1, 4):
            part = part + share[s] * vals[pl.ds(s * width, width), :]
        node_part[pl.ds(slot * (width + 8), width), :] = part
        node_part[pl.ds(slot * (width + 8) + width, 8), :] = jnp.full(
            (8, LANES), share[0] + share[1] + share[2] + share[3], F32
        )


def split_two(value):
    high = value.astype(BF16)
    low = (value - high.astype(F32)).astype(BF16)
    return jnp.concatenate([high, low], axis=1)


def mark_blocks(root_row, node_row, node_of, hot_root, hot_node, mask):
    blocks = hot_root.shape[0]
    chunk = min(blocks, 128)
    width = hot_node.shape[1]
    count = hot_root.shape[1]
    ones_root = jnp.ones((count, LANES), BF16)
    ones_node = jnp.ones((width, LANES), BF16)

    def body(i, state):
        at = aligned(i * chunk, chunk)
        here = lax.broadcasted_iota(jnp.int32, (chunk, count), 0) + at
        hot = (here == root_row[...]).astype(F32).astype(BF16)
        hot_root[pl.ds(at, chunk), :] = hot
        root_mask = jnp.dot(hot, ones_root, preferred_element_type=F32)
        here = lax.broadcasted_iota(jnp.int32, (chunk, width), 0) + at
        for s in range(4):
            hot = (here == node_row[pl.ds(node_of[s], 1), :]).astype(F32).astype(BF16)
            hot_node[pl.ds(aligned(s * blocks + at, chunk), chunk), :] = hot
            mask[pl.ds(4 * at + s, chunk, stride=4), :] = root_mask + jnp.dot(
                hot, ones_node, preferred_element_type=F32
            )
        return state

    lax.fori_loop(0, blocks // chunk, body, 0)


def fill_means(root_mean, node_mean, hot_root, hot_node, local_of, emit):
    blocks = hot_root.shape[0]
    chunk = min(blocks, 256)
    width = node_mean.shape[0] // 8
    root_rhs = split_two(root_mean[...])
    node_rhs = []
    for s in range(4):
        start = local_of[s] * width
        node_rhs.append(split_two(node_mean[pl.ds(start, width), :]))

    def body(i, state):
        at = aligned(i * chunk, chunk)
        got = jnp.dot(hot_root[pl.ds(at, chunk), :], root_rhs, preferred_element_type=F32)
        root_fill = got[:, :LANES] + got[:, LANES:]
        for s in range(4):
            hot = hot_node[pl.ds(aligned(s * blocks + at, chunk), chunk), :]
            got = jnp.dot(hot, node_rhs[s], preferred_element_type=F32)
            emit(
                pl.ds(4 * at + s, chunk, stride=4), root_fill + got[:, :LANES] + got[:, LANES:]
            )
        return state

    lax.fori_loop(0, blocks // chunk, body, 0)


def wait_bytes(ref, sem):
    pltpu.make_async_copy(ref, ref, sem).wait()


class Exchange:
    def __init__(self, ny, nx, nz, bufs, send, recv):
        (self.root_part, self.node_part, self.r0, self.n0, self.rsum, self.nsum, self.r1, self.n1,
         self.rz, self.r2, self.root_all, self.node_all) = bufs
        self.send, self.recv = send, recv
        sub, leaf = lax.axis_index("sub"), lax.axis_index("leaf")
        z, core = sub // 2, sub % 2
        y, x = leaf // nx, leaf % nx
        self.z, self.core, self.leaf, self.nz = z, core, leaf, nz
        self.cells = ny * nx
        self.chunk = self.rsum.shape[0] // self.cells
        self.rows = self.nsum.shape[0] // nz
        self.partner = {"sub": z * 2 + (1 - core), "leaf": leaf}
        self.plane, self.column = [], []
        for k in range(1, self.cells):
            other = ((y + k // nx) % ny) * nx + (x + k % nx) % nx
            self.plane.append((k, other, {"sub": sub, "leaf": other}))
        for k in range(1, nz):
            other = (z + k) % nz
            self.column.append((k, other, {"sub": other * 2 + core, "leaf": leaf}))
        self.peers = [self.partner] + [p[2] for p in self.plane] + [p[2] for p in self.column]

    def push(self, src, dst, which, peer):
        pltpu.make_async_remote_copy(
            src_ref=src, dst_ref=dst, send_sem=self.send.at[which], recv_sem=self.recv.at[which],
            device_id=peer, device_id_type=MESH,
        ).start()

    def root_to_partner(self):
        half = self.cells * self.chunk
        src = self.root_part.at[pl.ds(aligned((1 - self.core) * half), half)]
        self.push(src, self.r0, 1, self.partner)

    def node_to_partner(self):
        half = self.nz * self.rows
        src = self.node_part.at[pl.ds(aligned((1 - self.core) * half), half)]
        self.push(src, self.n0, 0, self.partner)

    def root_to_plane(self):
        half = self.cells * self.chunk
        wait_bytes(self.r0, self.recv.at[1])
        self.rsum[...] = self.root_part[pl.ds(aligned(self.core * half), half), :] + self.r0[...]
        for k, other, peer in self.plane:
            self.push(
                self.rsum.at[pl.ds(aligned(other * self.chunk), self.chunk)],
                self.r1.at[pl.ds((k - 1) * self.chunk, self.chunk)], 3, peer,
            )

    def node_to_column(self):
        half = self.nz * self.rows
        wait_bytes(self.n0, self.recv.at[0])
        self.nsum[...] = self.node_part[pl.ds(aligned(self.core * half), half), :] + self.n0[...]
        for k, other, peer in self.column:
            self.push(
                self.nsum.at[pl.ds(aligned(other * self.rows), self.rows)],
                self.n1.at[pl.ds((k - 1) * self.rows, self.rows)], 2, peer,
            )

    def node_back(self):
        width = self.rows - 8
        wait_bytes(self.n1, self.recv.at[2])
        acc = self.nsum[pl.ds(aligned(self.z * self.rows), self.rows), :]
        for k in range(1, self.nz):
            acc = acc + self.n1[pl.ds((k - 1) * self.rows, self.rows), :]
        spot = pl.ds(aligned((self.core * self.nz + self.z) * width), width)
        self.node_all[spot, :] = acc[:width] / acc[width:width + 1]
        for k, other, peer in self.column:
            self.push(self.node_all.at[spot], self.node_all.at[spot], 4, peer)

    def root_to_column(self):
        wait_bytes(self.r1, self.recv.at[3])
        acc = self.rsum[pl.ds(aligned(self.leaf * self.chunk), self.chunk), :]
        for k in range(1, self.cells):
            acc = acc + self.r1[pl.ds((k - 1) * self.chunk, self.chunk), :]
        self.rz[...] = acc
        for k, other, peer in self.column:
            self.push(self.rz, self.r2.at[pl.ds((k - 1) * self.chunk, self.chunk)], 5, peer)

    def root_back(self):
        keep = self.chunk - 8
        wait_bytes(self.r2, self.recv.at[5])
        total = self.rz[...]
        for k in range(1, self.nz):
            total = total + self.r2[pl.ds((k - 1) * self.chunk, self.chunk), :]
        spot = pl.ds(aligned((self.core * self.cells + self.leaf) * keep), keep)
        self.root_all[spot, :] = total[:keep] / total[keep:keep + 1]
        for k, other, peer in self.plane:
            self.push(self.root_all.at[spot], self.root_all.at[spot], 7, peer)

    def node_home(self):
        half = self.nz * (self.rows - 8)
        wait_bytes(self.node_all.at[pl.ds(0, half - (self.rows - 8))], self.recv.at[4])
        spot = self.node_all.at[pl.ds(aligned(self.core * half), half)]
        self.push(spot, spot, 6, self.partner)

    def root_home(self):
        keep = self.chunk - 8
        half = self.cells * keep
        wait_bytes(self.root_all.at[pl.ds(0, half - keep)], self.recv.at[7])
        spot = self.root_all.at[pl.ds(aligned(self.core * half), half)]
        self.push(spot, spot, 8, self.partner)

    def finish(self):
        wait_bytes(self.node_all.at[pl.ds(0, self.nz * (self.rows - 8))], self.recv.at[6])
        wait_bytes(self.root_all.at[pl.ds(0, self.cells * (self.chunk - 8))], self.recv.at[8])

    def drain(self):
        width, keep = self.rows - 8, self.chunk - 8
        sent = [
            self.n0, self.r0, self.n1, self.r1,
            self.node_all.at[pl.ds(0, (self.nz - 1) * width)],
            self.r2,
            self.node_all.at[pl.ds(0, self.nz * width)],
            self.root_all.at[pl.ds(0, (self.cells - 1) * keep)],
            self.root_all.at[pl.ds(0, self.cells * keep)],
        ]
        for which, ref in enumerate(sent):
            wait_bytes(ref, self.send.at[which])


def whole_kernel(
    chunks, most, ny, nx, nz,
    cols4, rows4, order, order4, follows, last4, inverse4, prob, node_of, local_of, root_blocks, node_blocks,
    tiles_hbm, cost, demand, upper, root_row, node_row,
    last, dual_rows, multiplier,
    tiles, field, wide, demand_f, demand_n, dual, sums, second, third, filled, mask, rest,
    total, vals, hot_root, hot_node, *others,
):
    bufs, (sems, send0, recv0, send1, recv1) = others[:24], others[24:]
    rounds = [
        Exchange(ny, nx, nz, bufs[:12], send0, recv0),
        Exchange(ny, nx, nz, bufs[12:], send1, recv1),
    ]
    start_tiles(tiles_hbm, tiles, sems, chunks)
    barrier = pltpu.get_barrier_semaphore()
    for peer in rounds[0].peers:
        pl.semaphore_signal(barrier, inc=1, device_id=peer, device_id_type=MESH)
    pairs = tiles.shape[0] // 2
    per_chunk = pairs // chunks
    rows = cost.shape[0]
    zero = jnp.zeros((8, LANES), F32)
    sums[pl.ds(PAD + 8 * pairs, 8), :] = zero

    spread_upper(upper, wide)
    demand_f[pl.ds(PAD, demand.shape[0]), :] = demand[...].astype(F32)
    first_step(cost, wide, field)

    def emit_first(p, image):
        want = pick_pair(demand_f, rows4[2 * p], rows4[2 * p + 1])
        demand_n[pl.ds(aligned(8 * p), 8), :] = want
        dual[pl.ds(aligned(PAD + 8 * p), 8), :] = jnp.maximum(0.25 * (want - image), 0.0)

    def emit_next(p, image):
        at = aligned(8 * p)
        old = dual[pl.ds(aligned(at + PAD), 8), :]
        dual[pl.ds(aligned(at + PAD), 8), :] = jnp.maximum(
            old + 0.25 * (demand_n[pl.ds(at, 8), :] - image), 0.0
        )

    def chunk_body(c, state):
        wait_tiles(tiles_hbm, tiles, sems, chunks, c)
        pairs_a(tiles, cols4, field, (c * per_chunk, per_chunk), emit_first, most)
        return state

    def forward(part):
        first, stop = part[0] * pairs // 8, part[1] * pairs // 8
        pairs_a(tiles, cols4, field, (first, stop - first), emit_next, most)

    def backward(part, carry):
        first, stop = part[0] * pairs // 8, part[1] * pairs // 8
        return transpose_pass(
            tiles, order, order4, follows, dual, sums, (first, stop - first), carry, most
        )

    lax.fori_loop(0, chunks, chunk_body, 0)
    backward((0, 8), zero)
    later_step(
        cost, wide, sums, last4, lambda at, before: before, second, field,
        lambda at: 0.5 * field[pl.ds(at + PAD, 16), :],
    )

    go = rounds[0]
    weigh_root(second, prob, root_blocks, total, go.root_part)
    pl.semaphore_wait(barrier, len(go.peers))
    go.root_to_partner()
    weigh_nodes(second, prob, node_of, local_of, node_blocks, vals, go.node_part)
    go.node_to_partner()
    go.root_to_plane()
    forward((0, 2))
    go.node_to_column()
    forward((2, 8))
    go.root_to_column()
    carry = backward((0, 2), zero)
    go.node_back()
    carry = backward((2, 6), carry)
    go.root_back()
    carry = backward((6, 8), carry)
    mark_blocks(root_row, node_row, node_of, hot_root, hot_node, mask)
    go.node_home()
    go.root_home()
    go.finish()

    def keep_means(at, means):
        filled[at, :] = means

    fill_means(go.root_all, go.node_all, hot_root, hot_node, local_of, keep_means)

    def consensus(at, before):
        return jnp.where(mask[pl.ds(at, 16), :] > 0.5, filled[pl.ds(at, 16), :], before)

    later_step(
        cost, wide, sums, last4, lambda at, before: 2.0 * consensus(at, before), third, field,
        lambda at: second[pl.ds(at, 16), :],
    )
    forward((0, 8))
    backward((0, 8), zero)

    def pull(at, before):
        start = second[pl.ds(at, 16), :]
        middle = consensus(at, start)
        return before - (start - middle) + middle

    later_step(
        cost, wide, sums, last4, pull, last, field, lambda at: third[pl.ds(at, 16), :],
    )

    go = rounds[1]
    weigh_root(last, prob, root_blocks, total, go.root_part)
    go.root_to_partner()
    weigh_nodes(last, prob, node_of, local_of, node_blocks, vals, go.node_part)
    go.node_to_partner()
    go.root_to_plane()
    forward((0, 2))
    go.node_to_column()
    forward((2, 8))
    go.root_to_column()

    def order_body(r, state):
        dual_rows[pl.ds(aligned(8 * r), 8), :] = pick_pair(
            dual, inverse4[2 * r], inverse4[2 * r + 1]
        )
        return state

    loop(pairs, 16, order_body)
    go.node_back()

    def rest_body(i, state):
        at = aligned(16 * i, 16)
        start = second[pl.ds(at, 16), :]
        rest[pl.ds(at, 16), :] = start - consensus(at, start) + last[pl.ds(at, 16), :]
        return state

    loop(rows // 16, 8, rest_body)
    go.root_back()
    go.node_home()
    go.root_home()
    go.finish()

    def update(at, means):
        multiplier[at, :] = jnp.where(mask[at, :] > 0.5, rest[at, :] - means, 0.0)

    fill_means(go.root_all, go.node_all, hot_root, hot_node, local_of, update)
    rounds[0].drain()
    rounds[1].drain()


def as_rows(field):
    count, size = field.shape
    return field.reshape(count, size // LANES, LANES).transpose(1, 0, 2).reshape(-1, LANES)


def from_rows(rows):
    blocks = rows.shape[0] // 4
    return rows.reshape(blocks, 4, LANES).transpose(1, 0, 2).reshape(4, blocks * LANES)


def per_device(
    tiles, tile_rows, tile_cols, cost, demand, upper, prob, node_of_scen, root_blocks, node_blocks
):
    nt = tiles.shape[0]
    nvt = cost.shape[1] // LANES
    nct = demand.shape[1] // LANES
    width = node_blocks.shape[1]
    root_count = root_blocks.shape[0]
    leaf = lax.axis_size("leaf")
    chunks = 4
    most = 64
    with jax.named_scope("tables"):
        n = jnp.arange(nt, dtype=jnp.int32)
        ahead = (tile_cols[None, :] < tile_cols[:, None]) | (
            (tile_cols[None, :] == tile_cols[:, None]) & (n[None, :] < n[:, None])
        )
        rank = jnp.sum(ahead.astype(jnp.int32), axis=1)
        place = rank[None, :] == n[:, None]
        order = jnp.sum(jnp.where(place, n[None, :], 0), axis=1)
        sorted_col = jnp.sum(jnp.where(place, tile_cols[None, :], 0), axis=1)
        follows = jnp.concatenate(
            [jnp.zeros((1,), F32), (sorted_col[1:] == sorted_col[:-1]).astype(F32)]
        )
        v = jnp.arange(nvt, dtype=jnp.int32)
        upto = jnp.sum((tile_cols[None, :] <= v[:, None]).astype(jnp.int32), axis=1)
        has = jnp.sum((tile_cols[None, :] == v[:, None]).astype(jnp.int32), axis=1)
        last4 = 4 * jnp.where(has > 0, upto - 1, nt)
        inverse4 = 4 * jnp.sum(
            jnp.where(tile_rows[None, :] == jnp.arange(nct)[:, None], n[None, :], 0), axis=1
        )
        cols4, rows4, order4 = 4 * tile_cols, 4 * tile_rows, 4 * order
    local_of = node_of_scen - 8 * lax.axis_index("leaf")
    cost_r, demand_r = as_rows(cost), as_rows(demand)
    upper_r = upper.reshape(nvt, LANES)
    root_row = root_blocks.reshape(1, root_count)
    sub = lax.axis_size("sub")
    nz = sub // 2
    ny = 4 if leaf == 16 else 1
    nx = leaf // ny
    chunk = root_count // (2 * leaf) + 8
    node_rows = width + 8
    pad_rows = PAD + 4 * nt + 16
    state_rows = 4 * nvt
    sm = pl.BlockSpec(memory_space=pltpu.SMEM)
    vm = pl.BlockSpec(memory_space=pltpu.VMEM)
    hbm = pl.BlockSpec(memory_space=pl.ANY)

    def lines(count):
        return pltpu.VMEM((count, LANES), F32)

    exchange = [
        lines(2 * leaf * chunk),
        lines(8 * node_rows),
        lines(leaf * chunk),
        lines(nz * node_rows),
        lines(leaf * chunk),
        lines(nz * node_rows),
        lines((leaf - 1) * chunk),
        lines((nz - 1) * node_rows),
        lines(chunk),
        lines((nz - 1) * chunk),
        lines(root_count),
        lines(8 * width),
    ]
    primal, dual, multiplier = pl.pallas_call(
        functools.partial(whole_kernel, chunks, most, ny, nx, nz),
        out_shape=[lines(state_rows), lines(4 * nct), lines(state_rows)],
        in_specs=[sm] * 12 + [hbm] + [vm] * 5,
        out_specs=[vm] * 3,
        scratch_shapes=[
            pltpu.VMEM(tiles.shape, BF16),
            lines(state_rows + 2 * PAD),
            lines(state_rows),
            lines(4 * nct + 2 * PAD),
            lines(4 * nt),
            lines(pad_rows),
            lines(pad_rows),
            lines(state_rows),
            lines(state_rows),
            lines(state_rows),
            lines(state_rows),
            lines(state_rows),
            lines(nvt),
            lines(4 * width),
            pltpu.VMEM((nvt, root_count), BF16),
            pltpu.VMEM((4 * nvt, width), BF16),
            *exchange,
            *exchange,
            pltpu.SemaphoreType.DMA((chunks,)),
            *[pltpu.SemaphoreType.DMA((9,))] * 4,
        ],
        compiler_params=pltpu.CompilerParams(
            collective_id=0, has_side_effects=True, vmem_limit_bytes=50 * 1024 * 1024
        ),
        name="hedging",
    )(
        cols4, rows4, order, order4, follows, last4, inverse4, prob, node_of_scen, local_of,
        root_blocks, node_blocks.reshape(-1), tiles, cost_r, demand_r, upper_r, root_row, node_blocks,
    )
    return from_rows(primal), from_rows(dual), from_rows(multiplier)


def solution(mesh):
    split = P(("sub", "leaf"), None)
    return jax.shard_map(
        per_device,
        mesh=mesh,
        in_specs=(
            P(), P(), P(), split, split, P(), P(("sub", "leaf")), P(("sub", "leaf")), P(), P(),
        ),
        out_specs=(split, split, split),
        check_vma=False,
    )
```

```python
import functools

import jax
import jax.numpy as jnp
from jax import lax
from jax.experimental import pallas as pl
from jax.experimental.pallas import tpu as pltpu
from jax.sharding import PartitionSpec as P

F32 = jnp.float32
BF16 = jnp.bfloat16
MESH = pl.DeviceIdType.MESH
LANES = 128
PAD = 8


def aligned(value, step=8):
    return pl.multiple_of(value, step)


def top_rows():
    return lax.broadcasted_iota(jnp.int32, (8, LANES), 0) < 4


def unroll_of(count, most):
    step = min(count, most)
    while count % step:
        step -= 1
    return step


def loop(count, most, body, carry=0, first=0):
    step = unroll_of(count, most)

    def outer(i, state):
        base = first + i * step
        return lax.fori_loop(0, step, lambda u, inner: body(base + u, inner), state, unroll=True)

    return lax.fori_loop(0, count // step, outer, carry)


def start_tiles(tiles_hbm, tiles, sems, chunks):
    size = tiles.shape[0] // chunks
    for c in range(chunks):
        part = pl.ds(c * size, size)
        pltpu.make_async_copy(tiles_hbm.at[part], tiles.at[part], sems.at[c]).start()


def wait_tiles(tiles_hbm, tiles, sems, chunks, c):
    size = tiles.shape[0] // chunks
    part = pl.ds(c * size, size)
    pltpu.make_async_copy(tiles_hbm.at[part], tiles.at[part], sems.at[c]).wait()


def pick_pair(ref, first4, second4):
    low = ref[pl.ds(first4 + PAD, 8), :]
    high = ref[pl.ds(second4 + (PAD - 4), 8), :]
    return jnp.where(top_rows(), low, high)


def spread_upper(upper, wide):
    blocks = upper.shape[0]
    for s in range(4):
        wide[pl.ds(s, blocks, stride=4), :] = upper[...]


def pairs_a(tiles, cols4, field, pairs, emit, most):
    def body(p, state):
        lhs = pick_pair(field, cols4[2 * p], cols4[2 * p + 1]).astype(BF16)
        rhs = tiles[pl.ds(2 * p, 2)].reshape(2 * LANES, LANES)
        both = lax.dot_general(lhs, rhs, (((1,), (1,)), ((), ())), preferred_element_type=F32)
        emit(p, jnp.where(top_rows(), both[:, :LANES], both[:, LANES:]))
        return state

    first, count = pairs
    loop(count, most, body, 0, first)


def transpose_pass(tiles, order, order4, follows, dual, sums, pairs, carry, most):
    def body(p, carry):
        a, b = 2 * p, 2 * p + 1
        top = top_rows()
        low = dual[pl.ds(order4[a] + PAD, 8), :]
        high = dual[pl.ds(order4[b] + (PAD - 4), 8), :]
        lhs = jnp.concatenate([jnp.where(top, low, 0.0), jnp.where(top, 0.0, high)], axis=1)
        rhs = jnp.concatenate([tiles[order[a]], tiles[order[b]]], axis=0)
        own = lax.dot_general(
            lhs.astype(BF16), rhs, (((1,), (0,)), ((), ())), preferred_element_type=F32
        )
        fa, fb = follows[a], follows[b]
        other = pltpu.roll(own, 4, 0)
        within = own + jnp.where(top, 0.0, fb) * other
        full = jnp.where(top, fb * own + other, within)
        both = fa * fb
        sums[pl.ds(aligned(PAD + 8 * p), 8), :] = within + jnp.where(top, fa, both) * carry
        return both * carry + full

    first, count = pairs
    return loop(count, most, body, carry, first)


def first_step(cost, wide, field):
    rows = cost.shape[0]

    def body(i, state):
        at = aligned(16 * i, 16)
        moved = -cost[pl.ds(at, 16), :].astype(F32) * 0.5
        field[pl.ds(at + PAD, 16), :] = 2.0 * jnp.clip(moved, 0.0, wide[pl.ds(at, 16), :])
        return state

    loop(rows // 16, 8, body)


def later_step(cost, wide, sums, last4, base, primal_out, field, old):
    rows = cost.shape[0]

    def body(i, state):
        at = aligned(16 * i, 16)
        gradient = jnp.concatenate(
            [
                pick_pair(sums, last4[4 * i], last4[4 * i + 1]),
                pick_pair(sums, last4[4 * i + 2], last4[4 * i + 3]),
            ],
            axis=0,
        )
        before = old(at)
        moved = base(at, before) - cost[pl.ds(at, 16), :].astype(F32) + gradient
        after = jnp.clip(moved * 0.5, 0.0, wide[pl.ds(at, 16), :])
        primal_out[pl.ds(at, 16), :] = after
        field[pl.ds(at + PAD, 16), :] = 2.0 * after - before
        return state

    loop(rows // 16, 8, body)


def weigh_root(primal, prob, root_blocks, total, root_part):
    blocks = total.shape[0]
    acc = prob[0] * primal[pl.ds(0, blocks, stride=4), :]
    for s in range(1, 4):
        acc = acc + prob[s] * primal[pl.ds(s, blocks, stride=4), :]
    total[...] = acc
    root_count = root_blocks.shape[0]
    pieces = (root_part.shape[0] - root_count) // 8
    each = root_count // pieces
    split = each + 8
    weight = jnp.full((8, LANES), prob[0] + prob[1] + prob[2] + prob[3], F32)

    def body(i, state):
        for u in range(each):
            root_part[pl.ds(i * split + u, 1), :] = total[pl.ds(root_blocks[i * each + u], 1), :]
        root_part[pl.ds(aligned(i * split + each), 8), :] = weight
        return state

    lax.fori_loop(0, pieces, body, 0)


def weigh_nodes(primal, prob, node_of, local_of, node_blocks, vals, node_part):
    width = node_part.shape[0] // 8 - 8
    for s in range(4):
        base = node_of[s] * width

        def body(b, state):
            row = primal[pl.ds(4 * node_blocks[base + b] + s, 1), :]
            vals[pl.ds(s * width + b, 1), :] = row
            return state

        loop(width, 16, body)
    for m in range(8):
        slot = m
        share = []
        for s in range(4):
            gap = local_of[s] - m
            share.append(prob[s] * (1 - jnp.minimum(gap * gap, 1)).astype(F32))
        part = share[0] * vals[pl.ds(0, width), :]
        for s in range(1, 4):
            part = part + share[s] * vals[pl.ds(s * width, width), :]
        node_part[pl.ds(slot * (width + 8), width), :] = part
        node_part[pl.ds(slot * (width + 8) + width, 8), :] = jnp.full(
            (8, LANES), share[0] + share[1] + share[2] + share[3], F32
        )


def split_two(value):
    high = value.astype(BF16)
    low = (value - high.astype(F32)).astype(BF16)
    return jnp.concatenate([high, low], axis=1)


def mark_blocks(root_row, node_row, node_of, hot_root, hot_node, mask):
    blocks = hot_root.shape[0]
    chunk = min(blocks, 128)
    width = hot_node.shape[1]
    count = hot_root.shape[1]
    ones_root = jnp.ones((count, LANES), BF16)
    ones_node = jnp.ones((width, LANES), BF16)

    def body(i, state):
        at = aligned(i * chunk, chunk)
        here = lax.broadcasted_iota(jnp.int32, (chunk, count), 0) + at
        hot = (here == root_row[...]).astype(F32).astype(BF16)
        hot_root[pl.ds(at, chunk), :] = hot
        root_mask = jnp.dot(hot, ones_root, preferred_element_type=F32)
        here = lax.broadcasted_iota(jnp.int32, (chunk, width), 0) + at
        for s in range(4):
            hot = (here == node_row[pl.ds(node_of[s], 1), :]).astype(F32).astype(BF16)
            hot_node[pl.ds(aligned(s * blocks + at, chunk), chunk), :] = hot
            mask[pl.ds(4 * at + s, chunk, stride=4), :] = root_mask + jnp.dot(
                hot, ones_node, preferred_element_type=F32
            )
        return state

    lax.fori_loop(0, blocks // chunk, body, 0)


def fill_means(root_mean, node_mean, hot_root, hot_node, local_of, emit):
    blocks = hot_root.shape[0]
    chunk = min(blocks, 256)
    width = node_mean.shape[0] // 8
    root_rhs = split_two(root_mean[...])
    node_rhs = []
    for s in range(4):
        start = local_of[s] * width
        node_rhs.append(split_two(node_mean[pl.ds(start, width), :]))

    def body(i, state):
        at = aligned(i * chunk, chunk)
        got = jnp.dot(hot_root[pl.ds(at, chunk), :], root_rhs, preferred_element_type=F32)
        root_fill = got[:, :LANES] + got[:, LANES:]
        for s in range(4):
            hot = hot_node[pl.ds(aligned(s * blocks + at, chunk), chunk), :]
            got = jnp.dot(hot, node_rhs[s], preferred_element_type=F32)
            emit(
                pl.ds(4 * at + s, chunk, stride=4), root_fill + got[:, :LANES] + got[:, LANES:]
            )
        return state

    lax.fori_loop(0, blocks // chunk, body, 0)


def wait_bytes(ref, sem):
    pltpu.make_async_copy(ref, ref, sem).wait()


class Exchange:
    def __init__(self, ny, nx, nz, bufs, send, recv):
        (self.root_part, self.node_part, self.n0, self.nsum, self.r1, self.n1,
         self.rz, self.r2, self.root_all, self.node_all) = bufs
        self.send, self.recv = send, recv
        sub, leaf = lax.axis_index("sub"), lax.axis_index("leaf")
        z, core = sub // 2, sub % 2
        y, x = leaf // nx, leaf % nx
        self.z, self.core, self.leaf, self.nz = z, core, leaf, nz
        self.cells = ny * nx
        self.chunk = self.rz.shape[0]
        self.rows = self.nsum.shape[0] // nz
        self.partner = {"sub": z * 2 + (1 - core), "leaf": leaf}
        self.plane, self.column = [], []
        for k in range(1, 2 * self.cells):
            cell = k % self.cells
            other = ((y + cell // nx) % ny) * nx + (x + cell % nx) % nx
            half = (core + k // self.cells) % 2
            self.plane.append((k, half * self.cells + other, {"sub": z * 2 + half, "leaf": other}))
        for k in range(1, nz):
            other = (z + k) % nz
            self.column.append((k, other, {"sub": other * 2 + core, "leaf": leaf}))
        self.peers = [p[2] for p in self.plane] + [p[2] for p in self.column]

    def push(self, src, dst, which, peer):
        pltpu.make_async_remote_copy(
            src_ref=src, dst_ref=dst, send_sem=self.send.at[which], recv_sem=self.recv.at[which],
            device_id=peer, device_id_type=MESH,
        ).start()

    def node_to_partner(self):
        half = self.nz * self.rows
        src = self.node_part.at[pl.ds(aligned((1 - self.core) * half), half)]
        self.push(src, self.n0, 0, self.partner)

    def root_to_plane(self):
        for k, place, peer in self.plane:
            self.push(
                self.root_part.at[pl.ds(aligned(place * self.chunk), self.chunk)],
                self.r1.at[pl.ds((k - 1) * self.chunk, self.chunk)], 1, peer,
            )

    def node_to_column(self):
        half = self.nz * self.rows
        wait_bytes(self.n0, self.recv.at[0])
        self.nsum[...] = self.node_part[pl.ds(aligned(self.core * half), half), :] + self.n0[...]
        for k, other, peer in self.column:
            self.push(
                self.nsum.at[pl.ds(aligned(other * self.rows), self.rows)],
                self.n1.at[pl.ds((k - 1) * self.rows, self.rows)], 2, peer,
            )

    def node_back(self):
        width = self.rows - 8
        wait_bytes(self.n1, self.recv.at[2])
        acc = self.nsum[pl.ds(aligned(self.z * self.rows), self.rows), :]
        for k in range(1, self.nz):
            acc = acc + self.n1[pl.ds((k - 1) * self.rows, self.rows), :]
        spot = pl.ds(aligned((self.core * self.nz + self.z) * width), width)
        self.node_all[spot, :] = acc[:width] / acc[width:width + 1]
        for k, other, peer in self.column:
            self.push(self.node_all.at[spot], self.node_all.at[spot], 4, peer)

    def root_to_column(self):
        wait_bytes(self.r1, self.recv.at[1])
        place = self.core * self.cells + self.leaf
        acc = self.root_part[pl.ds(aligned(place * self.chunk), self.chunk), :]
        for k in range(1, 2 * self.cells):
            acc = acc + self.r1[pl.ds((k - 1) * self.chunk, self.chunk), :]
        self.rz[...] = acc
        for k, other, peer in self.column:
            self.push(self.rz, self.r2.at[pl.ds((k - 1) * self.chunk, self.chunk)], 5, peer)

    def root_back(self):
        keep = self.chunk - 8
        wait_bytes(self.r2, self.recv.at[5])
        total = self.rz[...]
        for k in range(1, self.nz):
            total = total + self.r2[pl.ds((k - 1) * self.chunk, self.chunk), :]
        spot = pl.ds(aligned((self.core * self.cells + self.leaf) * keep), keep)
        self.root_all[spot, :] = total[:keep] / total[keep:keep + 1]
        for k, place, peer in self.plane:
            self.push(self.root_all.at[spot], self.root_all.at[spot], 3, peer)

    def node_home(self):
        half = self.nz * (self.rows - 8)
        wait_bytes(self.node_all.at[pl.ds(0, half - (self.rows - 8))], self.recv.at[4])
        spot = self.node_all.at[pl.ds(aligned(self.core * half), half)]
        self.push(spot, spot, 6, self.partner)

    def finish(self):
        keep = self.chunk - 8
        wait_bytes(self.node_all.at[pl.ds(0, self.nz * (self.rows - 8))], self.recv.at[6])
        wait_bytes(self.root_all.at[pl.ds(0, (2 * self.cells - 1) * keep)], self.recv.at[3])

    def drain(self):
        width, keep = self.rows - 8, self.chunk - 8
        sent = [
            self.n0, self.r1, self.n1,
            self.root_all.at[pl.ds(0, (2 * self.cells - 1) * keep)],
            self.node_all.at[pl.ds(0, (self.nz - 1) * width)],
            self.r2,
            self.node_all.at[pl.ds(0, self.nz * width)],
        ]
        for which, ref in enumerate(sent):
            wait_bytes(ref, self.send.at[which])


def whole_kernel(
    chunks, most, ny, nx, nz,
    cols4, rows4, order, order4, follows, last4, inverse4, prob, node_of, local_of, root_blocks, node_blocks,
    tiles_hbm, cost, demand, upper, root_row, node_row,
    last, dual_rows, multiplier,
    tiles, field, wide, demand_f, demand_n, dual, sums, second, third, filled, mask, rest,
    total, vals, hot_root, hot_node, *others,
):
    bufs, (sems, send0, recv0, send1, recv1) = others[:20], others[20:]
    rounds = [
        Exchange(ny, nx, nz, bufs[:10], send0, recv0),
        Exchange(ny, nx, nz, bufs[10:], send1, recv1),
    ]
    start_tiles(tiles_hbm, tiles, sems, chunks)
    barrier = pltpu.get_barrier_semaphore()
    for peer in rounds[0].peers:
        pl.semaphore_signal(barrier, inc=1, device_id=peer, device_id_type=MESH)
    pairs = tiles.shape[0] // 2
    per_chunk = pairs // chunks
    rows = cost.shape[0]
    zero = jnp.zeros((8, LANES), F32)
    sums[pl.ds(PAD + 8 * pairs, 8), :] = zero

    spread_upper(upper, wide)
    demand_f[pl.ds(PAD, demand.shape[0]), :] = demand[...].astype(F32)
    first_step(cost, wide, field)

    def emit_first(p, image):
        want = pick_pair(demand_f, rows4[2 * p], rows4[2 * p + 1])
        demand_n[pl.ds(aligned(8 * p), 8), :] = want
        dual[pl.ds(aligned(PAD + 8 * p), 8), :] = jnp.maximum(0.25 * (want - image), 0.0)

    def emit_next(p, image):
        at = aligned(8 * p)
        old = dual[pl.ds(aligned(at + PAD), 8), :]
        dual[pl.ds(aligned(at + PAD), 8), :] = jnp.maximum(
            old + 0.25 * (demand_n[pl.ds(at, 8), :] - image), 0.0
        )

    def chunk_body(c, state):
        wait_tiles(tiles_hbm, tiles, sems, chunks, c)
        pairs_a(tiles, cols4, field, (c * per_chunk, per_chunk), emit_first, most)
        return state

    def forward(part):
        first, stop = part[0] * pairs // 8, part[1] * pairs // 8
        pairs_a(tiles, cols4, field, (first, stop - first), emit_next, most)

    def backward(part, carry):
        first, stop = part[0] * pairs // 8, part[1] * pairs // 8
        return transpose_pass(
            tiles, order, order4, follows, dual, sums, (first, stop - first), carry, most
        )

    lax.fori_loop(0, chunks, chunk_body, 0)
    backward((0, 8), zero)
    later_step(
        cost, wide, sums, last4, lambda at, before: before, second, field,
        lambda at: 0.5 * field[pl.ds(at + PAD, 16), :],
    )

    go = rounds[0]
    weigh_root(second, prob, root_blocks, total, go.root_part)
    pl.semaphore_wait(barrier, len(go.peers))
    go.root_to_plane()
    weigh_nodes(second, prob, node_of, local_of, node_blocks, vals, go.node_part)
    go.node_to_partner()
    forward((0, 2))
    go.node_to_column()
    forward((2, 8))
    go.root_to_column()
    carry = backward((0, 2), zero)
    go.node_back()
    carry = backward((2, 6), carry)
    go.root_back()
    carry = backward((6, 8), carry)
    mark_blocks(root_row, node_row, node_of, hot_root, hot_node, mask)
    go.node_home()
    go.finish()

    def keep_means(at, means):
        filled[at, :] = means

    fill_means(go.root_all, go.node_all, hot_root, hot_node, local_of, keep_means)

    def consensus(at, before):
        return jnp.where(mask[pl.ds(at, 16), :] > 0.5, filled[pl.ds(at, 16), :], before)

    later_step(
        cost, wide, sums, last4, lambda at, before: 2.0 * consensus(at, before), third, field,
        lambda at: second[pl.ds(at, 16), :],
    )
    forward((0, 8))
    backward((0, 8), zero)

    def pull(at, before):
        start = second[pl.ds(at, 16), :]
        middle = consensus(at, start)
        return before - (start - middle) + middle

    later_step(
        cost, wide, sums, last4, pull, last, field, lambda at: third[pl.ds(at, 16), :],
    )

    go = rounds[1]
    weigh_root(last, prob, root_blocks, total, go.root_part)
    go.root_to_plane()
    weigh_nodes(last, prob, node_of, local_of, node_blocks, vals, go.node_part)
    go.node_to_partner()
    forward((0, 2))
    go.node_to_column()
    forward((2, 8))
    go.root_to_column()

    def order_body(r, state):
        dual_rows[pl.ds(aligned(8 * r), 8), :] = pick_pair(
            dual, inverse4[2 * r], inverse4[2 * r + 1]
        )
        return state

    loop(pairs, 16, order_body)
    go.node_back()

    def rest_body(i, state):
        at = aligned(16 * i, 16)
        start = second[pl.ds(at, 16), :]
        rest[pl.ds(at, 16), :] = start - consensus(at, start) + last[pl.ds(at, 16), :]
        return state

    loop(rows // 16, 8, rest_body)
    go.root_back()
    go.node_home()
    go.finish()

    def update(at, means):
        multiplier[at, :] = jnp.where(mask[at, :] > 0.5, rest[at, :] - means, 0.0)

    fill_means(go.root_all, go.node_all, hot_root, hot_node, local_of, update)
    rounds[0].drain()
    rounds[1].drain()


def table_kernel(
    cols, rows, node_of, cols4, rows4, order, order4, follows, last4, inverse4, local_of
):
    nt, nvt, nct = cols.shape[1], last4.shape[1], inverse4.shape[1]
    local_of[...] = node_of[...] - 8 * lax.axis_index("leaf")
    cols4[...] = 4 * cols[...]
    rows4[...] = 4 * rows[...]

    def column(line):
        return jnp.transpose(jnp.broadcast_to(line.astype(F32), (LANES, nt)))

    def ramp(count, width, start):
        return (lax.broadcasted_iota(jnp.int32, (count, width), 1) + start).astype(F32)

    def parts(count):
        width = min(count, LANES)
        return [(k, width) for k in range(0, count, width)]

    col_c, row_c = column(cols[...]), column(rows[...])
    n_c = lax.broadcasted_iota(jnp.int32, (nt, LANES), 0).astype(F32)
    ahead = 0.0
    for k, width in parts(nt):
        other = jnp.broadcast_to(cols[:, k:k + width].astype(F32), (nt, width))
        mine = col_c[:, :width]
        tie = (other == mine) & (ramp(nt, width, k) < n_c[:, :width])
        ahead = ahead + ((other < mine) | tie).astype(F32)
    rank = jnp.dot(
        ahead.astype(BF16), jnp.ones((ahead.shape[1], LANES), BF16), preferred_element_type=F32
    )
    n_r = lax.broadcasted_iota(jnp.int32, (8, nt), 1)
    col_r = jnp.broadcast_to(cols[...], (8, nt))
    line = lax.broadcasted_iota(jnp.int32, (8, nt), 0)
    picks = jnp.where(
        line == 0, n_r >> 3, jnp.where(line == 1, n_r & 7, jnp.where(line == 2, col_r >> 3, col_r & 7))
    ).astype(F32).astype(BF16)

    def choose(match):
        return jnp.dot(picks, match.astype(F32).astype(BF16), preferred_element_type=F32)

    sorted_cols = []
    for k, width in parts(nt):
        got = choose(rank[:, :width] == ramp(nt, width, k))
        place = (8.0 * got[0:1] + got[1:2]).astype(jnp.int32)
        order[:, k:k + width] = place
        order4[:, k:k + width] = 4 * place
        sorted_cols.append(jnp.broadcast_to(8.0 * got[2:3] + got[3:4], (8, width)))
    here = jnp.concatenate(sorted_cols, axis=1)
    same = (here == pltpu.roll(here, 1, 1)) & (n_r > 0)
    follows[...] = same.astype(F32)[0:1]
    counts = []
    ones = jnp.ones((8, nt), BF16)
    for k, width in parts(nvt):
        upto = (col_c[:, :width] <= ramp(nt, width, k)).astype(F32).astype(BF16)
        counts.append(jnp.dot(ones, upto, preferred_element_type=F32))
    upto = jnp.concatenate(counts, axis=1)
    first = lax.broadcasted_iota(jnp.int32, (8, nvt), 1) == 0
    before = jnp.where(first, 0.0, pltpu.roll(upto, 1, 1))
    last = jnp.where(upto > before, upto - 1.0, float(nt))
    last4[...] = (4.0 * last).astype(jnp.int32)[0:1]
    for k, width in parts(nct):
        got = choose(row_c[:, :width] == ramp(nt, width, k))
        inverse4[:, k:k + width] = (32.0 * got[0:1] + 4.0 * got[1:2]).astype(jnp.int32)


def as_rows(field):
    count, size = field.shape
    return field.reshape(count, size // LANES, LANES).transpose(1, 0, 2).reshape(-1, LANES)


def from_rows(rows):
    blocks = rows.shape[0] // 4
    return rows.reshape(blocks, 4, LANES).transpose(1, 0, 2).reshape(4, blocks * LANES)


def per_device(
    tiles, tile_rows, tile_cols, cost, demand, upper, prob, node_of_scen, root_blocks, node_blocks
):
    nt = tiles.shape[0]
    nvt = cost.shape[1] // LANES
    nct = demand.shape[1] // LANES
    width = node_blocks.shape[1]
    root_count = root_blocks.shape[0]
    leaf = lax.axis_size("leaf")
    chunks = 4
    most = 64
    vm = pl.BlockSpec(memory_space=pltpu.VMEM)

    def line(count, dtype=jnp.int32):
        return jax.ShapeDtypeStruct((1, count), dtype)

    tables = pl.pallas_call(
        table_kernel,
        out_shape=[
            line(nt), line(nt), line(nt), line(nt), line(nt, F32), line(nvt), line(nct), line(4),
        ],
        in_specs=[vm] * 3,
        out_specs=[vm] * 8,
        name="tables",
    )(tile_cols.reshape(1, nt), tile_rows.reshape(1, nt), node_of_scen.reshape(1, 4))
    cols4, rows4, order, order4, follows, last4, inverse4, local_of = [
        table.reshape(-1) for table in tables
    ]
    cost_r, demand_r = as_rows(cost), as_rows(demand)
    upper_r = upper.reshape(nvt, LANES)
    root_row = root_blocks.reshape(1, root_count)
    sub = lax.axis_size("sub")
    nz = sub // 2
    ny = 4 if leaf == 16 else 1
    nx = leaf // ny
    chunk = root_count // (2 * leaf) + 8
    node_rows = width + 8
    pad_rows = PAD + 4 * nt + 16
    state_rows = 4 * nvt
    sm = pl.BlockSpec(memory_space=pltpu.SMEM)
    hbm = pl.BlockSpec(memory_space=pl.ANY)

    def lines(count):
        return pltpu.VMEM((count, LANES), F32)

    exchange = [
        lines(2 * leaf * chunk),
        lines(8 * node_rows),
        lines(nz * node_rows),
        lines(nz * node_rows),
        lines((2 * leaf - 1) * chunk),
        lines((nz - 1) * node_rows),
        lines(chunk),
        lines((nz - 1) * chunk),
        lines(root_count),
        lines(8 * width),
    ]
    primal, dual, multiplier = pl.pallas_call(
        functools.partial(whole_kernel, chunks, most, ny, nx, nz),
        out_shape=[lines(state_rows), lines(4 * nct), lines(state_rows)],
        in_specs=[sm] * 12 + [hbm] + [vm] * 5,
        out_specs=[vm] * 3,
        scratch_shapes=[
            pltpu.VMEM(tiles.shape, BF16),
            lines(state_rows + 2 * PAD),
            lines(state_rows),
            lines(4 * nct + 2 * PAD),
            lines(4 * nt),
            lines(pad_rows),
            lines(pad_rows),
            lines(state_rows),
            lines(state_rows),
            lines(state_rows),
            lines(state_rows),
            lines(state_rows),
            lines(nvt),
            lines(4 * width),
            pltpu.VMEM((nvt, root_count), BF16),
            pltpu.VMEM((4 * nvt, width), BF16),
            *exchange,
            *exchange,
            pltpu.SemaphoreType.DMA((chunks,)),
            *[pltpu.SemaphoreType.DMA((7,))] * 4,
        ],
        compiler_params=pltpu.CompilerParams(
            collective_id=0, has_side_effects=True, vmem_limit_bytes=50 * 1024 * 1024
        ),
        name="hedging",
    )(
        cols4, rows4, order, order4, follows, last4, inverse4, prob, node_of_scen, local_of,
        root_blocks, node_blocks.reshape(-1), tiles, cost_r, demand_r, upper_r, root_row, node_blocks,
    )
    return from_rows(primal), from_rows(dual), from_rows(multiplier)


def solution(mesh):
    split = P(("sub", "leaf"), None)
    return jax.shard_map(
        per_device,
        mesh=mesh,
        in_specs=(
            P(), P(), P(), split, split, P(), P(("sub", "leaf")), P(("sub", "leaf")), P(), P(),
        ),
        out_specs=(split, split, split),
        check_vma=False,
    )
```
